512 devices in a mesh: tiles: 128 (over z, y, core), rep: 4 (over x).
Axes of the slice: x: 4, y: 4, z: 16, core: 2. Of those that a mesh axis runs over, the one named last changes fastest.
Arguments:
- tiles: bfloat16 [1024, 64, 4096], P(('tiles', 'rep')), may hold values from -6 to 6
- block_one: int32 [1024], P(('tiles', 'rep')), may hold values from 0 to 127
- block_two: int32 [1024], P(('tiles', 'rep')), may hold values from 0 to 255
- block_three: int32 [1024], P(('tiles', 'rep')), may hold values from 0 to 15
- owner_map: int32 [128], replicated, may hold values from 0 to 127, each once
- u_one: float32 [32, 8192], P(None, 'tiles'), may hold values from -6 to 6
- u_two: bfloat16 [32, 16384], P(None, 'tiles'), may hold values from -6 to 6
- u_three: bfloat16 [32, 1024], replicated, may hold values from -6 to 6
Outputs:
- factor: float32 [32, 8192], P(None, 'tiles')
- tile_factor: bfloat16 [1024, 2048], P(('tiles', 'rep'))
The draws below stay inside these ranges and needn't reach their ends.
All inputs are finite; a program needn't handle non-finite values.
Results may differ from the reference program's by a relative error of at most 0.0081.
Values may be sent and summed in bfloat16 or wider, within the bound.
A program may use at most 64 MiB of HBM per device.

```python
import math
import jax
import jax.numpy as jnp
import numpy as np
from jax import lax

B = 64
R = 32
TILE_DEV = 2
NB3 = 16
ITERS = 1
NS_STEPS = 2
NB1 = 128
NB2 = 256
NROWS = 8192
NT = 1024


def draw_u_one(key, part):
    noise = jax.random.normal(jax.random.fold_in(key, 11), (R, NROWS), jnp.float32)
    signs = (jax.random.randint(jax.random.fold_in(key, 12), (R, 1), 0, 2) * 2 - 1).astype(jnp.float32)
    common = jax.random.normal(jax.random.fold_in(key, 13), (1, NROWS), jnp.float32)
    return jnp.clip(noise + signs * common, -6.0, 6.0).astype(jnp.float32)


def plant(array, key, least, top_value):
    longest = array.shape.index(max(array.shape))
    spots = []
    for shift in (0, 1):
        where = [jax.random.randint(jax.random.fold_in(key, axis), (), 0, length) for axis, length in enumerate(array.shape)]
        where[longest] = (where[longest] + shift) % array.shape[longest]
        spots.append(tuple(where))
    return array.at[spots[0]].set(least).at[spots[1]].set(top_value)


def shard_levels(rng, shape, cuts, smallest, largest):
    factor_of = 1.0
    for position, shards_of in cuts:
        draws = jax.random.uniform(jax.random.fold_in(jax.random.fold_in(rng, 6), position), (shards_of,), jnp.float32, smallest / len(cuts), largest / len(cuts))
        factor_of = factor_of * jnp.repeat(jnp.exp(draws), shape[position] // shards_of).reshape((-1,) + (1,) * (len(shape) - 1 - position))
    return factor_of


def rank_bounds(count, lean):
    portions = [(1 << 20) // math.isqrt(rank ** lean) + 1 for rank in range(1, count + 1)]
    scale = 1 + sum(portions) // (1 << 30)
    return np.cumsum(np.array([max(1, weight // scale) for weight in portions]))


def skewed_ids(stream_key, shape, amount, lean):
    table = rank_bounds(amount, lean)
    ticket = jax.random.randint(jax.random.fold_in(stream_key, 1), shape, 0, int(table[amount - 1]))
    grade = jnp.searchsorted(jnp.asarray(table, jnp.int32), ticket, side="right")
    return jax.random.permutation(jax.random.fold_in(stream_key, 2), amount)[grade].astype(jnp.int32)


def bell_draw(key, dims, spread, reach, cuts=(), kind=jnp.bfloat16):
    gain = shard_levels(key, dims, cuts, -0.22, 0.18) if cuts else 1.0
    array = jax.random.normal(key, dims, jnp.float32) * spread * gain
    return jnp.minimum(jnp.maximum(array, -reach), reach).astype(kind)


def setup_inputs(seed: int = 0) -> dict:
    streams_of = jax.random.split(jax.random.key(seed), 9)
    return {
        "tiles": bell_draw(streams_of[0], (NT, B, B * B), 1.0, 6.0, ((0, 512),)),
        "block_one": plant(skewed_ids(streams_of[1], (NT,), NB1, 1), jax.random.fold_in(streams_of[1], 3), 0, NB1 - 1).astype(jnp.int32),
        "block_two": plant(jax.random.randint(streams_of[2], (NT,), 0, NB2), jax.random.fold_in(streams_of[2], 1), 0, NB2 - 1).astype(jnp.int32),
        "block_three": plant(jax.random.randint(streams_of[3], (NT,), 0, NB3), jax.random.fold_in(streams_of[3], 1), 0, NB3 - 1).astype(jnp.int32),
        "owner_map": jax.random.permutation(streams_of[4], NB1).astype(jnp.int32),
        "u_one": draw_u_one(jax.random.fold_in(streams_of[8], 71), 0),
        "u_two": bell_draw(streams_of[6], (R, NB2 * B), 1.0, 6.0, ((1, 128),)),
        "u_three": bell_draw(streams_of[7], (R, NB3 * B), 1.0, 6.0),
    }


def pick(table, index, width):
    grid = table.reshape(table.shape[0], -1, width)
    return jnp.transpose(jnp.take(grid, index, axis=1), (1, 0, 2))

def orthonormal(rows):
    hi = lax.Precision.HIGHEST
    g0 = jnp.dot(rows, rows.T, precision=hi, preferred_element_type=jnp.float32)
    msq = jnp.trace(g0) / NROWS
    inv = 1.0 / jnp.sqrt(msq + 1e-06)
    x = rows * inv
    g = g0 * (inv * inv) / NROWS
    eye = jnp.eye(R, dtype=jnp.float32)
    for step in range(NS_STEPS):
        if step > 0:
            g = jnp.dot(x, x.T, precision=hi, preferred_element_type=jnp.float32) / NROWS
        x = jnp.dot(1.5 * eye - 0.5 * g, x, precision=hi, preferred_element_type=jnp.float32)
    return x

def reference(tiles, block_one, block_two, block_three, owner_map, u_one, u_two, u_three):
    hi = lax.Precision.HIGHEST
    count = tiles.shape[0]
    groups = count // TILE_DEV
    positions = jnp.take(owner_map, block_one).astype(jnp.int32)
    two_pick = pick(u_two, block_two, B).reshape(groups, TILE_DEV, R, B)
    three_pick = pick(u_three, block_three, B).reshape(groups, TILE_DEV, R, B)

    def product_group(args):
        cube, two, three = args
        cube = cube.reshape(TILE_DEV, B, B, B).astype(jnp.float32)
        first = jnp.einsum('tijk,tsk->tijs', cube, three.astype(jnp.float32), precision=hi).astype(jnp.bfloat16)
        second = jnp.einsum('tijs,trj->tirs', first.astype(jnp.float32), two.astype(jnp.float32), precision=hi)
        return second.reshape(TILE_DEV, B, R * R).astype(jnp.bfloat16)
    prods = lax.map(product_group, (tiles.reshape(groups, TILE_DEV, B, B * B), two_pick, three_pick))
    pos_groups = positions.reshape(groups, TILE_DEV)
    current = u_one
    for it in range(ITERS):
        blocks = pick(current.astype(jnp.bfloat16), positions, B).reshape(groups, TILE_DEV, R, B)

        def add_w(total, args):
            prod, blk = args
            return (total + jnp.einsum('tic,tri->rc', prod.astype(jnp.float32), blk.astype(jnp.float32), precision=hi), None)
        project, _ = lax.scan(add_w, jnp.zeros((R, R * R), jnp.float32), (prods, blocks))
        project = project.astype(jnp.bfloat16).astype(jnp.float32)

        def add_z(total, args):
            prod, pos = args
            z_tile = jnp.einsum('rc,tic->tri', project, prod.astype(jnp.float32), precision=hi)
            return (total.at[:, pos, :].add(jnp.transpose(z_tile, (1, 0, 2))), None)
        rows, _ = lax.scan(add_z, jnp.zeros((R, NB1, B), jnp.float32), (prods, pos_groups))
        current = orthonormal(rows.reshape(R, NB1 * B))
    tile_factor = pick(current.astype(jnp.bfloat16), positions, B).reshape(count, R * B)
    return (current, tile_factor)
```

```python
import functools

import jax
import jax.numpy as jnp
from jax import lax
from jax.experimental import pallas as pl
from jax.experimental.pallas import tpu as pltpu
from jax.sharding import PartitionSpec as P

MESH = pl.DeviceIdType.MESH
NS_STEPS = 2
YC = 8
F32 = jnp.float32
BF16 = jnp.bfloat16
HI = lax.Precision.HIGHEST


def iota(shape, dim):
    return lax.broadcasted_iota(jnp.int32, shape, dim)


def nt(a, b, precision=None):
    return lax.dot_general(
        a, b, (((1,), (1,)), ((), ())), precision=precision, preferred_element_type=F32
    )


def kernel(
    nx, nz, rows_total,
    tiles_ref, b1_ref, b2_ref, b3_ref, owner_ref, u1_ref, u2_ref, u3_ref,
    factor_ref, tf_ref,
    tl, us, shq, tq, req, reqs, obuf, gbuf, ft, pt, wsend, wrecv, lsend, lrecv, psend, precv,
    zsend, zrecv, ysend, yrecv, gsend, grecv, ssend, srecv, xsend, xrecv, mref,
    tsem, send, recv,
):
    pln = nx * YC
    per = nz // nx
    qr = 32 // nx
    t_id = lax.axis_index("tiles")
    x = lax.axis_index("rep")
    z = lax.div(t_id, YC)
    yc = lax.rem(t_id, YC)
    m = x * YC + yc

    copies = [
        pltpu.make_async_copy(tiles_ref.at[t], tl.at[pl.ds(64 * t, 64)], tsem.at[t])
        for t in range(2)
    ]
    for c in copies:
        c.start()

    def mate(k):
        w = lax.rem(m + k, pln)
        return w, {"tiles": z * YC + lax.rem(w, YC), "rep": lax.div(w, YC)}

    def peer(k):
        w = lax.rem(z + k, nz)
        return w, {"tiles": w * YC + yc, "rep": x}

    def xmate(k):
        w = lax.rem(x + k, nx)
        return w, {"tiles": t_id, "rep": w}

    barrier = pltpu.get_barrier_semaphore()

    def greet(who, n):
        def body(k, carry):
            pl.semaphore_signal(barrier, inc=1, device_id=who(k)[1], device_id_type=MESH)
            return carry

        lax.fori_loop(1, n, body, 0)

    greet(mate, pln)
    greet(peer, nz)

    def post(who, n, phase, src, dst):
        def body(k, carry):
            w, device = who(k)
            pltpu.make_async_remote_copy(
                src_ref=src(w), dst_ref=dst, send_sem=send.at[phase], recv_sem=recv.at[phase],
                device_id=device, device_id_type=MESH,
            ).start()
            return carry

        lax.fori_loop(1, n, body, 0)

    def land(buf, n, phase):
        part = buf.at[pl.ds(0, n - 1)]
        pltpu.make_async_copy(part, part, recv.at[phase]).wait()

    def sent(buf, n, phase):
        part = buf.at[pl.ds(0, n - 1)]
        pltpu.make_async_copy(part, part, send.at[phase]).wait()

    b2 = [b2_ref[t] for t in range(2)]
    b3 = [b3_ref[t] for t in range(2)]
    pos = [owner_ref[b1_ref[t]] for t in range(2)]

    r16 = iota((16, 128), 0)
    l16 = iota((16, 128), 1)

    def ask(q0, q1):
        want = jnp.where(r16 < qr, q0 * qr, q1 * qr - qr) + r16
        return jnp.where(l16 == want, 1.0, 0.0).astype(BF16)

    reqs[pl.ds(0, 16), :] = ask(lax.shift_right_logical(b2[0], 4), lax.shift_right_logical(b2[1], 4))
    reqs[pl.ds(16, 16), :] = ask(lax.shift_right_logical(pos[0], 3), lax.shift_right_logical(pos[1], 3))
    reqs[pl.ds(32, 16), :] = jnp.where(l16 < 64, pos[0], pos[1]).astype(F32).astype(BF16)
    us[:, pl.ds(0, 128)] = u2_ref[...].astype(F32)
    us[:, pl.ds(128, 64)] = u1_ref[...]
    us[:, pl.ds(192, 64)] = jnp.zeros((32, 64), F32)
    shq[...] = us[pl.ds(pl.multiple_of(x * qr, qr), qr), :].astype(BF16)

    pl.semaphore_wait(barrier, pln + nz - 2)
    post(peer, nz, 0, lambda w: shq, tq.at[z])
    post(mate, pln, 1, lambda w: reqs, req.at[m])
    tq[z] = shq[...]
    req[m] = reqs[...]

    lane128 = iota((32, 128), 1)
    spread = jnp.where(iota((256, 32), 0) // 8 == iota((256, 32), 1), 1.0, 0.0).astype(BF16)
    diag = []
    for t in range(2):
        chunk = jnp.zeros((32, 128), F32)
        for q in range(8):
            part = u3_ref[:, q * 128 : (q + 1) * 128].astype(F32)
            chunk = chunk + jnp.where(lax.shift_right_logical(b3[t], 1) == q, part, 0.0)
        swapped = pltpu.roll(chunk, 64, 1)
        odd = lax.rem(b3[t], 2) == 1
        twice = jnp.where((lane128 < 64) != odd, chunk, swapped)
        wide = jnp.dot(spread, twice.astype(BF16), preferred_element_type=F32)
        row = lax.rem(iota((256, 128), 0), 8)
        half = jnp.where(iota((256, 128), 1) < 64, 0, 1)
        diag.append(
            jnp.concatenate(
                [jnp.where(row == half + 2 * q, wide, 0.0).astype(BF16) for q in range(4)], axis=1
            )
        )
    for c in copies:
        c.wait()
    low256 = iota((256, 128), 1) < 64
    for jc in range(8):
        block = tl[:, jc * 512 : (jc + 1) * 512]
        out = jnp.where(low256, nt(diag[0], block), nt(diag[1], block))
        ft[:, jc * 8 : (jc + 1) * 8, :] = out.reshape(32, 8, 128)

    land(tq, nz, 0)
    land(req, pln, 1)
    table = tq[...].astype(F32).reshape(nz * qr, 256).astype(BF16)
    two_part = jnp.dot(
        req[:, 0:16, :].reshape(pln * 16, 128), table[:, 0:128], preferred_element_type=F32
    )
    one_part = jnp.dot(
        req[:, 16:32, :].reshape(pln * 16, 128), table[:, 128:256], preferred_element_type=F32
    )
    obuf[:, 0:16, :] = two_part.reshape(pln, 16, 128).astype(BF16)
    obuf[:, 16:32, :] = one_part.reshape(pln, 16, 128).astype(BF16)
    post(mate, pln, 2, lambda w: obuf.at[w], gbuf.at[m])
    gbuf[m] = obuf[m]
    land(gbuf, pln, 2)

    r32 = iota((32, 128), 0)
    holder = jnp.where(
        r32 < 16,
        jnp.where(r32 < 8, lax.rem(lax.shift_right_logical(b2[0], 1), YC),
                  lax.rem(lax.shift_right_logical(b2[1], 1), YC)),
        jnp.where(r32 < 24, lax.rem(pos[0], YC), lax.rem(pos[1], YC)),
    )
    parts = []
    for xx in range(nx):
        acc = jnp.zeros((32, 128), F32)
        for cc in range(YC):
            acc = acc + jnp.where(holder == cc, gbuf[xx * YC + cc].astype(F32), 0.0)
        parts.append(acc)

    def rows_of(slot):
        return jnp.concatenate([p[slot * 8 : slot * 8 + 8] for p in parts], axis=0)

    low = lane128 < 64
    two = []
    for t in range(2):
        v = rows_of(t)
        two.append(jnp.where(lax.rem(b2[t], 2) == 1, pltpu.roll(v, 64, 1), v))
    u2 = jnp.concatenate(two, axis=0)[:, 0:64].astype(BF16)
    readers = jnp.where(low, rows_of(2), pltpu.roll(rows_of(3), 64, 1)).astype(BF16)

    for s in range(32):
        d = jnp.dot(u2, ft[s].astype(BF16), preferred_element_type=F32)
        pt[s * 32 : (s + 1) * 32, :] = jnp.where(low, d[0:32], d[32:64]).astype(BF16)

    w_part = nt(readers, pt[...])
    for q in range(8):
        wsend[:, q, :] = w_part[:, q * 128 : (q + 1) * 128]
    post(mate, pln, 3, lambda w: wsend.at[w], wrecv.at[m])
    wrecv[m] = wsend[m]
    land(wrecv, pln, 3)
    lsend[...] = jnp.sum(wrecv[...], axis=0)
    post(peer, nz, 4, lambda w: lsend, lrecv.at[z])
    lrecv[z] = lsend[...]
    land(lrecv, nz, 4)
    psend[...] = jnp.sum(lrecv[...], axis=0).astype(BF16).astype(F32)
    post(mate, pln, 5, lambda w: psend, precv.at[m])
    precv[m] = psend[...]
    land(precv, pln, 5)
    project = jnp.concatenate([precv[:, q, :].astype(BF16) for q in range(8)], axis=1)

    zsend[...] = jnp.dot(project, pt[...], preferred_element_type=F32).astype(BF16)
    post(mate, pln, 6, lambda w: zsend, zrecv.at[m])
    zrecv[m] = zsend[...]
    land(zrecv, pln, 6)
    sums = [jnp.zeros((32, 128), F32) for _ in range(per)]
    where_to = []
    for w in range(pln):
        goes = req[w, 32:48, :].astype(F32)[0:8]
        goes = jnp.concatenate([goes] * 4, axis=0)
        where_to.append(goes)
        val = zrecv[w].astype(F32)
        for k in range(per):
            mine = ((x * per + k) * YC + yc).astype(F32)
            sums[k] = sums[k] + jnp.where(goes == mine, val, 0.0)
    sums = [v + pltpu.roll(v, 64, 1) for v in sums]
    for k in range(0, per, 2):
        ysend[:, k * 64 : k * 64 + 128] = jnp.where(low, sums[k], sums[k + 1]).astype(BF16)
    post(peer, nz, 7, lambda w: ysend, yrecv.at[z])
    yrecv[z] = ysend[...]
    land(yrecv, nz, 7)
    total = yrecv[0].astype(F32)
    for w in range(1, nz):
        total = total + yrecv[w].astype(F32)

    gw = nt(total, jnp.concatenate([total] * 4, axis=0), HI)
    lane8 = lax.shift_right_logical(iota((8, 128), 1), 5)
    packed = jnp.zeros((8, 128), F32)
    for q in range(4):
        packed = packed + jnp.where(lane8 == q, gw[q * 8 : q * 8 + 8], 0.0)
    gsend[...] = packed
    post(mate, pln, 8, lambda w: gsend, grecv.at[m])
    grecv[m] = packed
    blocks = []
    for k in range(per):
        pair = total[:, (k // 2) * 128 : (k // 2) * 128 + 128]
        other = pltpu.roll(pair, 64, 1)
        blocks.append(jnp.where(low, pair, other) if k % 2 == 0 else jnp.where(low, other, pair))
    for w in range(pln):
        val = jnp.zeros((32, 128), F32)
        for k in range(per):
            mine = ((x * per + k) * YC + yc).astype(F32)
            val = val + jnp.where(where_to[w] == mine, blocks[k], 0.0)
        ssend[w] = val.astype(BF16)
    post(mate, pln, 9, lambda w: ssend.at[w], srecv.at[m])
    srecv[m] = ssend[m]
    own = jnp.zeros((32, 128), F32)
    for k in range(per):
        own = own + jnp.where(lax.rem(z, per) == k, blocks[k], 0.0)
    xsend[...] = own
    post(xmate, nx, 10, lambda w: xsend, xrecv.at[x])
    xrecv[x] = own

    land(grecv, pln, 8)
    packed = jnp.sum(grecv[...], axis=0)
    tall = jnp.concatenate([jnp.where(lane8 == q, packed, 0.0) for q in range(4)], axis=0)
    fold = jnp.where(
        jnp.bitwise_and(iota((128, 32), 0), 31) == iota((128, 32), 1), 1.0, 0.0
    )
    g0 = jnp.dot(tall, fold, precision=HI, preferred_element_type=F32)
    eye = jnp.where(iota((32, 32), 0) == iota((32, 32), 1), 1.0, 0.0)
    trace = jnp.sum(jnp.sum(g0 * eye, axis=1, keepdims=True), axis=0, keepdims=True)
    inv = 1.0 / jnp.sqrt(trace / rows_total + 1e-06)
    g = g0 * (inv * inv) / rows_total
    move = eye * inv
    for step in range(NS_STEPS):
        if step > 0:
            g = jnp.dot(
                jnp.dot(a, g, precision=HI, preferred_element_type=F32), a,
                precision=HI, preferred_element_type=F32,
            )
        a = 1.5 * eye - 0.5 * g
        move = jnp.dot(a, move, precision=HI, preferred_element_type=F32)
    mref[:, 0:32] = move

    land(srecv, pln, 9)
    land(xrecv, nx, 10)
    got = srecv[0].astype(F32)
    for w in range(1, pln):
        got = got + srecv[w].astype(F32)
    mine = xrecv[lax.div(z, per)]
    factor_ref[...] = jnp.dot(move, mine[:, 0:64], precision=HI, preferred_element_type=F32)
    order = jnp.concatenate(
        [mref[pl.ds(0, 16, stride=2), :][:, 0:32], mref[pl.ds(1, 16, stride=2), :][:, 0:32]], axis=0
    )
    other = pltpu.roll(got, 64, 1)
    low16 = iota((16, 128), 1) < 64
    for t in range(2):
        both = jnp.where(low, got, other) if t == 0 else jnp.where(low, other, got)
        v = jnp.dot(order, both, precision=HI, preferred_element_type=F32)
        tf_ref[t] = jnp.where(low16, v[0:16], v[16:32]).astype(BF16)

    sent(tq, nz, 0)
    sent(req, pln, 1)
    sent(gbuf, pln, 2)
    sent(wrecv, pln, 3)
    sent(lrecv, nz, 4)
    sent(precv, pln, 5)
    sent(zrecv, pln, 6)
    sent(yrecv, nz, 7)
    sent(grecv, pln, 8)
    sent(srecv, pln, 9)
    sent(xrecv, nx, 10)


def solution(mesh):
    nx = mesh.shape["rep"]
    nz = mesh.shape["tiles"] // YC
    pln = nx * YC
    qr = 32 // nx
    per = nz // nx

    def per_device(tiles, block_one, block_two, block_three, owner_map, u_one, u_two, u_three):
        rows_total = owner_map.shape[0] * tiles.shape[1]
        vm = pl.BlockSpec(memory_space=pltpu.VMEM)
        sm = pl.BlockSpec(memory_space=pltpu.SMEM)
        factor, tf = pl.pallas_call(
            functools.partial(kernel, nx, nz, rows_total),
            out_shape=(
                jax.ShapeDtypeStruct((32, 64), F32),
                jax.ShapeDtypeStruct((2, 16, 128), BF16),
            ),
            in_specs=[pl.BlockSpec(memory_space=pl.ANY), sm, sm, sm, sm, vm, vm, vm],
            out_specs=(vm, vm),
            scratch_shapes=[
                pltpu.VMEM((128, 4096), BF16),
                pltpu.VMEM((32, 256), F32),
                pltpu.VMEM((qr, 256), BF16),
                pltpu.VMEM((nz, qr, 256), BF16),
                pltpu.VMEM((pln, 48, 128), BF16),
                pltpu.VMEM((48, 128), BF16),
                pltpu.VMEM((pln, 32, 128), BF16),
                pltpu.VMEM((pln, 32, 128), BF16),
                pltpu.VMEM((32, 64, 128), F32),
                pltpu.VMEM((1024, 128), BF16),
                pltpu.VMEM((pln, 8, 128), F32),
                pltpu.VMEM((pln, 8, 128), F32),
                pltpu.VMEM((8, 128), F32),
                pltpu.VMEM((nz, 8, 128), F32),
                pltpu.VMEM((8, 128), F32),
                pltpu.VMEM((pln, 8, 128), F32),
                pltpu.VMEM((32, 128), BF16),
                pltpu.VMEM((pln, 32, 128), BF16),
                pltpu.VMEM((32, 64 * per), BF16),
                pltpu.VMEM((nz, 32, 64 * per), BF16),
                pltpu.VMEM((8, 128), F32),
                pltpu.VMEM((pln, 8, 128), F32),
                pltpu.VMEM((pln, 32, 128), BF16),
                pltpu.VMEM((pln, 32, 128), BF16),
                pltpu.VMEM((32, 128), F32),
                pltpu.VMEM((nx, 32, 128), F32),
                pltpu.VMEM((32, 128), F32),
                pltpu.SemaphoreType.DMA((2,)),
                pltpu.SemaphoreType.DMA((11,)),
                pltpu.SemaphoreType.DMA((11,)),
            ],
            compiler_params=pltpu.CompilerParams(
                collective_id=0, has_side_effects=True, vmem_limit_bytes=32 << 20
            ),
            name="hooi_step",
        )(tiles, block_one, block_two, block_three, owner_map, u_one, u_two, u_three)
        return factor, tf.reshape(2, 2048)

    in_specs = (
        P(("tiles", "rep"), None, None),
        P(("tiles", "rep")),
        P(("tiles", "rep")),
        P(("tiles", "rep")),
        P(),
        P(None, "tiles"),
        P(None, "tiles"),
        P(),
    )
    out_specs = (P(None, "tiles"), P(("tiles", "rep"), None))
    return jax.shard_map(
        per_device, mesh=mesh, in_specs=in_specs, out_specs=out_specs, check_vma=False
    )
```

```python
import functools

import jax
import jax.numpy as jnp
from jax import lax
from jax.experimental import pallas as pl
from jax.experimental.pallas import tpu as pltpu
from jax.sharding import PartitionSpec as P

MESH = pl.DeviceIdType.MESH
NS_STEPS = 2
YC = 8
F32 = jnp.float32
BF16 = jnp.bfloat16
HI = lax.Precision.HIGHEST


def iota(shape, dim):
    return lax.broadcasted_iota(jnp.int32, shape, dim)


def nt(a, b, precision=None):
    return lax.dot_general(
        a, b, (((1,), (1,)), ((), ())), precision=precision, preferred_element_type=F32
    )


def kernel(
    nx, nz, rows_total,
    tiles_ref, b1_hbm, b2_hbm, b3_hbm, owner_hbm, u1_hbm, u2_hbm, u3_hbm,
    factor_ref, tf_ref,
    b1_ref, b2_ref, b3_ref, owner_ref, u1_ref, u2_ref, u3_ref,
    tl, us, shq, tq, req, reqs, obuf, gbuf, ft, pt, wsend, wrecv, lsend, lrecv, psend, precv,
    zsend, zrecv, goes, ysend, yrecv, yall, gsend, grecv, ssend, srecv, xsend, xrecv, mref,
    tsem, send, recv,
):
    pln = nx * YC
    per = nz // nx
    qr = 32 // nx
    t_id = lax.axis_index("tiles")
    x = lax.axis_index("rep")
    z = lax.div(t_id, YC)
    yc = lax.rem(t_id, YC)
    m = x * YC + yc

    copies = [
        pltpu.make_async_copy(tiles_ref.at[t], tl.at[pl.ds(64 * t, 64)], tsem.at[t])
        for t in range(2)
    ]
    inputs = [
        pltpu.make_async_copy(src, dst, tsem.at[2 + n])
        for n, (src, dst) in enumerate(
            ((b1_hbm, b1_ref), (owner_hbm, owner_ref), (b2_hbm, b2_ref), (u2_hbm, u2_ref),
             (u1_hbm, u1_ref), (b3_hbm, b3_ref), (u3_hbm, u3_ref))
        )
    ]
    for c in inputs + copies:
        c.start()

    def mate(k):
        w = lax.rem(m + k, pln)
        return w, {"tiles": z * YC + lax.rem(w, YC), "rep": lax.div(w, YC)}

    def peer(k):
        w = lax.rem(z + k, nz)
        return w, {"tiles": w * YC + yc, "rep": x}

    def xmate(k):
        w = lax.rem(x + k, nx)
        return w, {"tiles": t_id, "rep": w}

    barrier = pltpu.get_barrier_semaphore()

    def greet(who, n):
        def body(k, carry):
            pl.semaphore_signal(barrier, inc=1, device_id=who(k)[1], device_id_type=MESH)
            return carry

        lax.fori_loop(1, n, body, 0)

    greet(mate, pln)
    greet(peer, nz)

    def post(who, n, phase, src, dst):
        def body(k, carry):
            w, device = who(k)
            pltpu.make_async_remote_copy(
                src_ref=src(w), dst_ref=dst, send_sem=send.at[phase], recv_sem=recv.at[phase],
                device_id=device, device_id_type=MESH,
            ).start()
            return carry

        lax.fori_loop(1, n, body, 0)

    def land(buf, n, phase):
        part = buf.at[pl.ds(0, n - 1)]
        pltpu.make_async_copy(part, part, recv.at[phase]).wait()

    def sent(buf, n, phase):
        part = buf.at[pl.ds(0, n - 1)]
        pltpu.make_async_copy(part, part, send.at[phase]).wait()

    for c in inputs:
        c.wait()
    b2 = [b2_ref[t] for t in range(2)]
    b3 = [b3_ref[t] for t in range(2)]
    pos = [owner_ref[b1_ref[t]] for t in range(2)]

    r16 = iota((16, 128), 0)
    l16 = iota((16, 128), 1)

    def ask(q0, q1):
        want = jnp.where(r16 < qr, q0 * qr, q1 * qr - qr) + r16
        return jnp.where(l16 == want, 1.0, 0.0).astype(BF16)

    reqs[pl.ds(0, 16), :] = ask(lax.shift_right_logical(b2[0], 4), lax.shift_right_logical(b2[1], 4))
    reqs[pl.ds(16, 16), :] = ask(lax.shift_right_logical(pos[0], 3), lax.shift_right_logical(pos[1], 3))
    us[:, pl.ds(0, 128)] = u2_ref[...].astype(F32)
    us[:, pl.ds(128, 64)] = u1_ref[...]
    us[:, pl.ds(192, 64)] = jnp.zeros((32, 64), F32)
    shq[...] = us[pl.ds(pl.multiple_of(x * qr, qr), qr), :].astype(BF16)

    pl.semaphore_wait(barrier, pln + nz - 2)
    post(peer, nz, 0, lambda w: shq, tq.at[z])
    post(mate, pln, 1, lambda w: reqs, req.at[m])
    tq[z] = shq[...]
    req[m] = reqs[...]

    lane128 = iota((32, 128), 1)
    spread = jnp.where(iota((256, 32), 0) // 8 == iota((256, 32), 1), 1.0, 0.0).astype(BF16)
    diag = []
    for t in range(2):
        chunk = jnp.zeros((32, 128), F32)
        for q in range(8):
            part = u3_ref[:, q * 128 : (q + 1) * 128].astype(F32)
            chunk = chunk + jnp.where(lax.shift_right_logical(b3[t], 1) == q, part, 0.0)
        swapped = pltpu.roll(chunk, 64, 1)
        odd = lax.rem(b3[t], 2) == 1
        twice = jnp.where((lane128 < 64) != odd, chunk, swapped)
        wide = jnp.dot(spread, twice.astype(BF16), preferred_element_type=F32)
        row = lax.rem(iota((256, 128), 0), 8)
        half = jnp.where(iota((256, 128), 1) < 64, 0, 1)
        diag.append(
            jnp.concatenate(
                [jnp.where(row == half + 2 * q, wide, 0.0).astype(BF16) for q in range(4)], axis=1
            )
        )
    for c in copies:
        c.wait()
    low256 = iota((256, 128), 1) < 64
    for jc in range(8):
        block = tl[:, jc * 512 : (jc + 1) * 512]
        out = jnp.where(low256, nt(diag[0], block), nt(diag[1], block))
        ft[:, jc * 8 : (jc + 1) * 8, :] = out.reshape(32, 8, 128)

    land(tq, nz, 0)
    land(req, pln, 1)
    table = tq[...].astype(F32).reshape(nz * qr, 256).astype(BF16)
    two_part = jnp.dot(
        req[:, 0:16, :].reshape(pln * 16, 128), table[:, 0:128], preferred_element_type=F32
    )
    one_part = jnp.dot(
        req[:, 16:32, :].reshape(pln * 16, 128), table[:, 128:256], preferred_element_type=F32
    )
    obuf[:, 0:16, :] = two_part.reshape(pln, 16, 128).astype(BF16)
    at = jnp.where(r16 < 8, pos[0], pos[1]).astype(F32)
    one_part = jnp.where(l16 < 64, one_part.reshape(pln, 16, 128), at)
    obuf[:, 16:32, :] = one_part.astype(BF16)
    post(mate, pln, 2, lambda w: obuf.at[w], gbuf.at[m])
    gbuf[m] = obuf[m]
    land(gbuf, pln, 2)

    r32 = iota((32, 128), 0)
    holder = jnp.where(
        r32 < 16,
        jnp.where(r32 < 8, lax.rem(lax.shift_right_logical(b2[0], 1), YC),
                  lax.rem(lax.shift_right_logical(b2[1], 1), YC)),
        jnp.where(r32 < 24, lax.rem(pos[0], YC), lax.rem(pos[1], YC)),
    )
    low8 = iota((8, 128), 1) < 64
    parts = []
    for xx in range(nx):
        acc = jnp.zeros((32, 128), F32)
        for cc in range(YC):
            val = gbuf[xx * YC + cc].astype(F32)
            goes[xx * YC + cc] = jnp.where(low8, pltpu.roll(val[16:24], 64, 1), val[24:32])
            acc = acc + jnp.where(holder == cc, val, 0.0)
        parts.append(acc)

    def rows_of(slot):
        return jnp.concatenate([p[slot * 8 : slot * 8 + 8] for p in parts], axis=0)

    low = lane128 < 64
    two = []
    for t in range(2):
        v = rows_of(t)
        two.append(jnp.where(lax.rem(b2[t], 2) == 1, pltpu.roll(v, 64, 1), v))
    u2 = jnp.concatenate(two, axis=0)[:, 0:64].astype(BF16)
    readers = jnp.where(low, rows_of(2), pltpu.roll(rows_of(3), 64, 1)).astype(BF16)

    for s in range(32):
        d = jnp.dot(u2, ft[s].astype(BF16), preferred_element_type=F32)
        pt[s * 32 : (s + 1) * 32, :] = jnp.where(low, d[0:32], d[32:64]).astype(BF16)

    w_part = nt(readers, pt[...])
    for q in range(8):
        wsend[:, q, :] = w_part[:, q * 128 : (q + 1) * 128]
    post(mate, pln, 3, lambda w: wsend.at[w], wrecv.at[m])
    wrecv[m] = wsend[m]
    land(wrecv, pln, 3)
    lsend[...] = jnp.sum(wrecv[...], axis=0)
    post(peer, nz, 4, lambda w: lsend, lrecv.at[z])
    lrecv[z] = lsend[...]
    land(lrecv, nz, 4)
    psend[...] = jnp.sum(lrecv[...], axis=0).astype(BF16).astype(F32)
    post(mate, pln, 5, lambda w: psend, precv.at[m])
    precv[m] = psend[...]
    land(precv, pln, 5)
    project = jnp.concatenate([precv[:, q, :].astype(BF16) for q in range(8)], axis=1)

    zsend[...] = jnp.dot(project, pt[...], preferred_element_type=F32).astype(BF16)
    post(mate, pln, 6, lambda w: zsend, zrecv.at[m])
    zrecv[m] = zsend[...]
    land(zrecv, pln, 6)
    mine = [((x * per + k) * YC + yc).astype(F32) for k in range(per)]
    sums = [jnp.zeros((4, 8, 128), F32) for _ in range(per)]
    for w in range(pln):
        to = goes[w]
        val = zrecv[w].astype(F32).reshape(4, 8, 128)
        sums = [v + jnp.where((to == p)[None], val, 0.0) for v, p in zip(sums, mine)]
    sums = [v.reshape(32, 128) for v in sums]
    sums = [v + pltpu.roll(v, 64, 1) for v in sums]
    half = per // 2
    for h in range(half):
        ysend[:, h, :] = jnp.where(low, sums[2 * h], sums[2 * h + 1])
    rz = 32 // nz

    def slab(ref, w):
        return ref.at[pl.ds(w * rz, rz)]

    post(peer, nz, 7, lambda w: slab(ysend, w), yrecv.at[z])
    yrecv[z] = ysend[pl.ds(z * rz, rz)]
    land(yrecv, nz, 7)
    yall[pl.ds(z * rz, rz)] = jnp.sum(yrecv[...], axis=0)
    post(peer, nz, 11, lambda w: slab(yall, z), slab(yall, z))
    part = yall.at[pl.ds(0, rz * (nz - 1))]
    pltpu.make_async_copy(part, part, recv.at[11]).wait()
    total = jnp.concatenate([yall[:, h, :] for h in range(half)], axis=1)

    gw = nt(total, jnp.concatenate([total] * 4, axis=0), HI)
    lane8 = lax.shift_right_logical(iota((8, 128), 1), 5)
    packed = jnp.zeros((8, 128), F32)
    for q in range(4):
        packed = packed + jnp.where(lane8 == q, gw[q * 8 : q * 8 + 8], 0.0)
    gsend[...] = packed
    post(mate, pln, 8, lambda w: gsend, grecv.at[m])
    grecv[m] = packed
    blocks = []
    for k in range(per):
        pair = total[:, (k // 2) * 128 : (k // 2) * 128 + 128]
        other = pltpu.roll(pair, 64, 1)
        blocks.append(jnp.where(low, pair, other) if k % 2 == 0 else jnp.where(low, other, pair))
    blocks = [v.reshape(4, 8, 128) for v in blocks]

    def answer(w):
        to = goes[w]
        val = jnp.zeros((4, 8, 128), F32)
        for v, p in zip(blocks, mine):
            val = val + jnp.where((to == p)[None], v, 0.0)
        return val.reshape(32, 128).astype(BF16)

    def reply(k, carry):
        w, device = mate(k)
        ssend[w] = answer(w)
        pltpu.make_async_remote_copy(
            src_ref=ssend.at[w], dst_ref=srecv.at[m], send_sem=send.at[9], recv_sem=recv.at[9],
            device_id=device, device_id_type=MESH,
        ).start()
        return carry

    lax.fori_loop(1, pln, reply, 0)
    srecv[m] = answer(m)
    own = jnp.zeros((32, 128), F32)
    for k in range(per):
        own = own + jnp.where(lax.rem(z, per) == k, blocks[k].reshape(32, 128), 0.0)
    xsend[...] = own
    post(xmate, nx, 10, lambda w: xsend, xrecv.at[x])
    xrecv[x] = own

    land(grecv, pln, 8)
    packed = jnp.sum(grecv[...], axis=0)
    tall = jnp.concatenate([jnp.where(lane8 == q, packed, 0.0) for q in range(4)], axis=0)
    fold = jnp.where(
        jnp.bitwise_and(iota((128, 32), 0), 31) == iota((128, 32), 1), 1.0, 0.0
    )
    g0 = jnp.dot(tall, fold, precision=HI, preferred_element_type=F32)
    eye = jnp.where(iota((32, 32), 0) == iota((32, 32), 1), 1.0, 0.0)
    trace = jnp.sum(jnp.sum(g0 * eye, axis=1, keepdims=True), axis=0, keepdims=True)
    inv = 1.0 / jnp.sqrt(trace / rows_total + 1e-06)
    g = g0 * (inv * inv) / rows_total
    move = eye * inv
    for step in range(NS_STEPS):
        if step > 0:
            g = jnp.dot(
                jnp.dot(a, g, precision=HI, preferred_element_type=F32), a,
                precision=HI, preferred_element_type=F32,
            )
        a = 1.5 * eye - 0.5 * g
        move = jnp.dot(a, move, precision=HI, preferred_element_type=F32)
    mref[:, 0:32] = move

    land(srecv, pln, 9)
    land(xrecv, nx, 10)
    got = srecv[0].astype(F32)
    for w in range(1, pln):
        got = got + srecv[w].astype(F32)
    held = xrecv[lax.div(z, per)]
    factor_ref[...] = jnp.dot(move, held[:, 0:64], precision=HI, preferred_element_type=F32)
    order = jnp.concatenate(
        [mref[pl.ds(0, 16, stride=2), :][:, 0:32], mref[pl.ds(1, 16, stride=2), :][:, 0:32]], axis=0
    )
    other = pltpu.roll(got, 64, 1)
    low16 = iota((16, 128), 1) < 64
    for t in range(2):
        both = jnp.where(low, got, other) if t == 0 else jnp.where(low, other, got)
        v = jnp.dot(order, both, precision=HI, preferred_element_type=F32)
        tf_ref[t] = jnp.where(low16, v[0:16], v[16:32]).astype(BF16)

    sent(tq, nz, 0)
    sent(req, pln, 1)
    sent(gbuf, pln, 2)
    sent(wrecv, pln, 3)
    sent(lrecv, nz, 4)
    sent(precv, pln, 5)
    sent(zrecv, pln, 6)
    sent(yrecv, nz, 7)
    pltpu.make_async_copy(part, part, send.at[11]).wait()
    sent(grecv, pln, 8)
    sent(srecv, pln, 9)
    sent(xrecv, nx, 10)


def solution(mesh):
    nx = mesh.shape["rep"]
    nz = mesh.shape["tiles"] // YC
    pln = nx * YC
    qr = 32 // nx
    per = nz // nx

    def per_device(tiles, block_one, block_two, block_three, owner_map, u_one, u_two, u_three):
        rows_total = owner_map.shape[0] * tiles.shape[1]
        vm = pl.BlockSpec(memory_space=pltpu.VMEM)
        factor, tf = pl.pallas_call(
            functools.partial(kernel, nx, nz, rows_total),
            out_shape=(
                jax.ShapeDtypeStruct((32, 64), F32),
                jax.ShapeDtypeStruct((2, 16, 128), BF16),
            ),
            in_specs=[pl.BlockSpec(memory_space=pltpu.HBM)] * 8,
            out_specs=(vm, vm),
            scratch_shapes=[
                pltpu.SMEM((2,), jnp.int32),
                pltpu.SMEM((2,), jnp.int32),
                pltpu.SMEM((2,), jnp.int32),
                pltpu.SMEM((owner_map.shape[0],), jnp.int32),
                pltpu.VMEM(u_one.shape, F32),
                pltpu.VMEM(u_two.shape, BF16),
                pltpu.VMEM(u_three.shape, BF16),
                pltpu.VMEM((128, 4096), BF16),
                pltpu.VMEM((32, 256), F32),
                pltpu.VMEM((qr, 256), BF16),
                pltpu.VMEM((nz, qr, 256), BF16),
                pltpu.VMEM((pln, 32, 128), BF16),
                pltpu.VMEM((32, 128), BF16),
                pltpu.VMEM((pln, 32, 128), BF16),
                pltpu.VMEM((pln, 32, 128), BF16),
                pltpu.VMEM((32, 64, 128), F32),
                pltpu.VMEM((1024, 128), BF16),
                pltpu.VMEM((pln, 8, 128), F32),
                pltpu.VMEM((pln, 8, 128), F32),
                pltpu.VMEM((8, 128), F32),
                pltpu.VMEM((nz, 8, 128), F32),
                pltpu.VMEM((8, 128), F32),
                pltpu.VMEM((pln, 8, 128), F32),
                pltpu.VMEM((32, 128), BF16),
                pltpu.VMEM((pln, 32, 128), BF16),
                pltpu.VMEM((pln, 8, 128), F32),
                pltpu.VMEM((32, per // 2, 128), F32),
                pltpu.VMEM((nz, 32 // nz, per // 2, 128), F32),
                pltpu.VMEM((32, per // 2, 128), F32),
                pltpu.VMEM((8, 128), F32),
                pltpu.VMEM((pln, 8, 128), F32),
                pltpu.VMEM((pln, 32, 128), BF16),
                pltpu.VMEM((pln, 32, 128), BF16),
                pltpu.VMEM((32, 128), F32),
                pltpu.VMEM((nx, 32, 128), F32),
                pltpu.VMEM((32, 128), F32),
                pltpu.SemaphoreType.DMA((9,)),
                pltpu.SemaphoreType.DMA((12,)),
                pltpu.SemaphoreType.DMA((12,)),
            ],
            compiler_params=pltpu.CompilerParams(
                collective_id=0, has_side_effects=True, vmem_limit_bytes=60 << 20
            ),
            name="hooi_step",
        )(tiles, block_one, block_two, block_three, owner_map, u_one, u_two, u_three)
        return factor, tf.reshape(2, 2048)

    in_specs = (
        P(("tiles", "rep"), None, None),
        P(("tiles", "rep")),
        P(("tiles", "rep")),
        P(("tiles", "rep")),
        P(),
        P(None, "tiles"),
        P(None, "tiles"),
        P(),
    )
    out_specs = (P(None, "tiles"), P(("tiles", "rep"), None))
    return jax.shard_map(
        per_device, mesh=mesh, in_specs=in_specs, out_specs=out_specs, check_vma=False
    )
```

```python
import functools

import jax
import jax.numpy as jnp
from jax import lax
from jax.experimental import pallas as pl
from jax.experimental.pallas import tpu as pltpu
from jax.sharding import PartitionSpec as P

MESH = pl.DeviceIdType.MESH
NS_STEPS = 2
YC = 8
F32 = jnp.float32
BF16 = jnp.bfloat16
HI = lax.Precision.HIGHEST


def iota(shape, dim):
    return lax.broadcasted_iota(jnp.int32, shape, dim)


def nt(a, b, precision=None):
    return lax.dot_general(
        a, b, (((1,), (1,)), ((), ())), precision=precision, preferred_element_type=F32
    )


def kernel(
    nx, nz, rows_total,
    tiles_ref, b1_hbm, b2_hbm, b3_hbm, owner_hbm, u1_hbm, u2_hbm, u3_hbm,
    factor_ref, tf_ref,
    b1_ref, b2_ref, b3_ref, owner_ref, u1_ref, u2_ref, u3_ref,
    tl, us, shq, tq, req, reqs, obuf, gbuf, ft, pt, wsend, wrecv, lsend, lrecv, psend, precv,
    zsend, zrecv, gosend, goes, ysend, yrecv, yall, gsend, grecv, ssend, srecv, xsend, xrecv, mref,
    tsem, send, recv,
):
    pln = nx * YC
    per = nz // nx
    qr = 32 // nx
    t_id = lax.axis_index("tiles")
    x = lax.axis_index("rep")
    z = lax.div(t_id, YC)
    yc = lax.rem(t_id, YC)
    m = x * YC + yc

    copies = [
        pltpu.make_async_copy(tiles_ref.at[t], tl.at[pl.ds(64 * t, 64)], tsem.at[t])
        for t in range(2)
    ]
    inputs = [
        pltpu.make_async_copy(src, dst, tsem.at[2 + n])
        for n, (src, dst) in enumerate(
            ((u2_hbm, u2_ref), (u1_hbm, u1_ref), (b1_hbm, b1_ref), (owner_hbm, owner_ref),
             (b2_hbm, b2_ref), (b3_hbm, b3_ref), (u3_hbm, u3_ref))
        )
    ]
    for c in inputs + copies:
        c.start()

    def far(d, n):
        return min(d, n - d)

    xs = [lax.rem(x + d, nx) for d in range(nx)]
    ys = [lax.rem(lax.div(yc, 2) + d, YC // 2) * 2 for d in range(YC // 2)]
    cs = [lax.rem(yc, 2), 1 - lax.rem(yc, 2)]
    steps = [
        (far(dx, nx) + far(dy, YC // 2), dx, dy, dc)
        for dx in range(nx) for dy in range(YC // 2) for dc in range(2)
    ]
    steps = sorted(steps, reverse=True)[:-1]
    mates = [
        (xs[dx] * YC + ys[dy] + cs[dc], {"tiles": z * YC + ys[dy] + cs[dc], "rep": xs[dx]})
        for _, dx, dy, dc in steps
    ]
    zs = [lax.rem(z + d, nz) for d in sorted(range(1, nz), key=lambda d: -far(d, nz))]
    peers = [(w, {"tiles": w * YC + yc, "rep": x}) for w in zs]
    xmates = [(w, {"tiles": t_id, "rep": w}) for w in xs[1:]]

    barrier = pltpu.get_barrier_semaphore()
    for _, device in peers + mates:
        pl.semaphore_signal(barrier, inc=1, device_id=device, device_id_type=MESH)

    def post(who, phase, src, dst):
        for w, device in who:
            pltpu.make_async_remote_copy(
                src_ref=src(w), dst_ref=dst, send_sem=send.at[phase], recv_sem=recv.at[phase],
                device_id=device, device_id_type=MESH,
            ).start()

    def land(buf, n, phase):
        part = buf.at[pl.ds(0, n - 1)]
        pltpu.make_async_copy(part, part, recv.at[phase]).wait()

    def sent(buf, n, phase):
        part = buf.at[pl.ds(0, n - 1)]
        pltpu.make_async_copy(part, part, send.at[phase]).wait()

    for c in inputs[:2]:
        c.wait()
    us[:, pl.ds(0, 128)] = u2_ref[...].astype(F32)
    us[:, pl.ds(128, 64)] = jnp.zeros((32, 64), F32)
    us[:, pl.ds(192, 64)] = u1_ref[...]
    shq[...] = us[pl.ds(pl.multiple_of(x * qr, qr), qr), :].astype(BF16)
    pl.semaphore_wait(barrier, pln + nz - 2)
    post(peers, 0, lambda w: shq, tq.at[z])

    for c in inputs[2:]:
        c.wait()
    b2 = [b2_ref[t] for t in range(2)]
    b3 = [b3_ref[t] for t in range(2)]
    pos = [owner_ref[b1_ref[t]] for t in range(2)]

    r16 = iota((16, 128), 0)
    l16 = iota((16, 128), 1)

    def ask(q0, q1):
        want = jnp.where(r16 < qr, q0 * qr, q1 * qr - qr) + r16
        return jnp.where(l16 == want, 1.0, 0.0)

    ask_two = ask(lax.shift_right_logical(b2[0], 4), lax.shift_right_logical(b2[1], 4))
    odd = jnp.where(r16 < qr, lax.rem(b2[0], 2), lax.rem(b2[1], 2)) == 1
    reqs[:, 0:128] = jnp.where(odd, 0.0, ask_two).astype(BF16)
    reqs[:, 128:256] = jnp.where(odd, ask_two, 0.0).astype(BF16)
    reqs[:, 256:384] = ask(
        lax.shift_right_logical(pos[0], 3), lax.shift_right_logical(pos[1], 3)
    ).astype(BF16)
    post(mates, 1, lambda w: reqs, req.at[m])
    tq[z] = shq[...]
    req[m] = reqs[...]
    gosend[...] = jnp.where(iota((8, 128), 1) < 64, pos[0], pos[1]).astype(F32)
    goes[m] = gosend[...]

    lane128 = iota((32, 128), 1)
    spread = jnp.where(iota((256, 32), 0) // 8 == iota((256, 32), 1), 1.0, 0.0).astype(BF16)
    diag = []
    for t in range(2):
        chunk = jnp.zeros((32, 128), F32)
        for q in range(8):
            part = u3_ref[:, q * 128 : (q + 1) * 128].astype(F32)
            chunk = chunk + jnp.where(lax.shift_right_logical(b3[t], 1) == q, part, 0.0)
        swapped = pltpu.roll(chunk, 64, 1)
        odd = lax.rem(b3[t], 2) == 1
        twice = jnp.where((lane128 < 64) != odd, chunk, swapped)
        wide = jnp.dot(spread, twice.astype(BF16), preferred_element_type=F32)
        row = lax.rem(iota((256, 128), 0), 8)
        half = jnp.where(iota((256, 128), 1) < 64, 0, 1)
        diag.append(
            jnp.concatenate(
                [jnp.where(row == half + 2 * q, wide, 0.0).astype(BF16) for q in range(4)], axis=1
            )
        )
    for c in copies:
        c.wait()
    low256 = iota((256, 128), 1) < 64
    for jc in range(8):
        block = tl[:, jc * 512 : (jc + 1) * 512]
        out = jnp.where(low256, nt(diag[0], block), nt(diag[1], block))
        ft[:, jc * 8 : (jc + 1) * 8, :] = out.reshape(32, 8, 128)

    land(tq, nz, 0)
    land(req, pln, 1)
    table = tq[...].astype(F32).reshape(nz * qr, 256)
    halves = jnp.concatenate([table[:, 0:128], pltpu.roll(table[:, 0:128], 64, 1)], axis=0)
    two_part = jnp.dot(
        req[:, :, 0:256].reshape(pln * 16, 256), halves.astype(BF16), preferred_element_type=F32
    )
    one_part = jnp.dot(
        req[:, :, 256:384].reshape(pln * 16, 128), table[:, 128:256].astype(BF16),
        preferred_element_type=F32,
    )
    both = jnp.where(iota((pln * 16, 128), 1) < 64, two_part, one_part)
    obuf[...] = both.reshape(pln, 16, 128).astype(BF16)
    post(mates, 2, lambda w: obuf.at[w], gbuf.at[m])
    gbuf[m] = obuf[m]
    land(gbuf, pln, 2)

    held_two = [lax.rem(lax.shift_right_logical(b, 1), YC) for b in b2]
    held_one = [lax.rem(p, YC) for p in pos]
    holder = jnp.where(
        l16 < 64,
        jnp.where(r16 < 8, held_two[0], held_two[1]),
        jnp.where(r16 < 8, held_one[0], held_one[1]),
    )
    parts = []
    for xx in range(nx):
        acc = jnp.zeros((16, 128), F32)
        for cc in range(YC):
            acc = acc + jnp.where(holder == cc, gbuf[xx * YC + cc].astype(F32), 0.0)
        parts.append(acc)
    low = lane128 < 64
    picked = [jnp.concatenate([p[t * 8 : t * 8 + 8] for p in parts], axis=0) for t in range(2)]
    u2 = jnp.concatenate(picked, axis=0)[:, 0:64].astype(BF16)
    readers = jnp.where(low, pltpu.roll(picked[0], 64, 1), picked[1]).astype(BF16)

    for s in range(32):
        d = jnp.dot(u2, ft[s].astype(BF16), preferred_element_type=F32)
        pt[s * 32 : (s + 1) * 32, :] = jnp.where(low, d[0:32], d[32:64]).astype(BF16)

    w_part = nt(readers, pt[...])
    for q in range(8):
        wsend[:, q, :] = w_part[:, q * 128 : (q + 1) * 128]
    post(mates, 3, lambda w: wsend.at[w], wrecv.at[m])
    wrecv[m] = wsend[m]
    land(wrecv, pln, 3)
    lsend[...] = jnp.sum(wrecv[...], axis=0)
    post(peers, 4, lambda w: lsend, lrecv.at[z])
    lrecv[z] = lsend[...]
    post(mates, 12, lambda w: gosend, goes.at[m])
    land(lrecv, nz, 4)
    psend[...] = jnp.sum(lrecv[...], axis=0).astype(BF16).astype(F32)
    post(mates, 5, lambda w: psend, precv.at[m])
    precv[m] = psend[...]
    land(precv, pln, 5)
    project = jnp.concatenate([precv[:, q, :].astype(BF16) for q in range(8)], axis=1)

    zsend[...] = jnp.dot(project, pt[...], preferred_element_type=F32).astype(BF16)
    post(mates, 6, lambda w: zsend, zrecv.at[m])
    zrecv[m] = zsend[...]
    land(zrecv, pln, 6)
    mine = [((x * per + k) * YC + yc).astype(F32) for k in range(per)]
    land(goes, pln, 12)
    sums = [jnp.zeros((4, 8, 128), F32) for _ in range(per)]
    for w in range(pln):
        to = goes[w]
        val = zrecv[w].astype(F32).reshape(4, 8, 128)
        sums = [v + jnp.where((to == p)[None], val, 0.0) for v, p in zip(sums, mine)]
    sums = [v.reshape(32, 128) for v in sums]
    sums = [v + pltpu.roll(v, 64, 1) for v in sums]
    half = per // 2
    for h in range(half):
        ysend[:, h, :] = jnp.where(low, sums[2 * h], sums[2 * h + 1])
    rz = 32 // nz

    def slab(ref, w):
        return ref.at[pl.ds(w * rz, rz)]

    post(peers, 7, lambda w: slab(ysend, w), yrecv.at[z])
    yrecv[z] = ysend[pl.ds(z * rz, rz)]
    land(yrecv, nz, 7)
    yall[pl.ds(z * rz, rz)] = jnp.sum(yrecv[...], axis=0)
    post(peers, 11, lambda w: slab(yall, z), slab(yall, z))
    part = yall.at[pl.ds(0, rz * (nz - 1))]
    pltpu.make_async_copy(part, part, recv.at[11]).wait()
    total = jnp.concatenate([yall[:, h, :] for h in range(half)], axis=1)

    gw = nt(total, jnp.concatenate([total] * 4, axis=0), HI)
    lane8 = lax.shift_right_logical(iota((8, 128), 1), 5)
    packed = jnp.zeros((8, 128), F32)
    for q in range(4):
        packed = packed + jnp.where(lane8 == q, gw[q * 8 : q * 8 + 8], 0.0)
    gsend[...] = packed
    post(mates, 8, lambda w: gsend, grecv.at[m])
    grecv[m] = packed
    blocks = []
    for k in range(per):
        pair = total[:, (k // 2) * 128 : (k // 2) * 128 + 128]
        other = pltpu.roll(pair, 64, 1)
        blocks.append(jnp.where(low, pair, other) if k % 2 == 0 else jnp.where(low, other, pair))
    blocks = [v.reshape(4, 8, 128) for v in blocks]

    def answer(w):
        to = goes[w]
        val = jnp.zeros((4, 8, 128), F32)
        for v, p in zip(blocks, mine):
            val = val + jnp.where((to == p)[None], v, 0.0)
        return val.reshape(32, 128).astype(BF16)

    for w, device in mates:
        ssend[w] = answer(w)
        pltpu.make_async_remote_copy(
            src_ref=ssend.at[w], dst_ref=srecv.at[m], send_sem=send.at[9], recv_sem=recv.at[9],
            device_id=device, device_id_type=MESH,
        ).start()
    srecv[m] = answer(m)
    own = jnp.zeros((32, 128), F32)
    for k in range(per):
        own = own + jnp.where(lax.rem(z, per) == k, blocks[k].reshape(32, 128), 0.0)
    xsend[...] = jnp.where(low[0:16], own[0:16], own[16:32])
    post(xmates, 10, lambda w: xsend, xrecv.at[x])
    xrecv[x] = xsend[...]

    land(grecv, pln, 8)
    packed = jnp.sum(grecv[...], axis=0)
    tall = jnp.concatenate([jnp.where(lane8 == q, packed, 0.0) for q in range(4)], axis=0)
    fold = jnp.where(
        jnp.bitwise_and(iota((128, 32), 0), 31) == iota((128, 32), 1), 1.0, 0.0
    )
    g0 = jnp.dot(tall, fold, precision=HI, preferred_element_type=F32)
    eye = jnp.where(iota((32, 32), 0) == iota((32, 32), 1), 1.0, 0.0)
    trace = jnp.sum(jnp.sum(g0 * eye, axis=1, keepdims=True), axis=0, keepdims=True)
    inv = 1.0 / jnp.sqrt(trace / rows_total + 1e-06)
    g = g0 * (inv * inv) / rows_total
    move = eye * inv
    for step in range(NS_STEPS):
        if step > 0:
            g = jnp.dot(
                jnp.dot(a, g, precision=HI, preferred_element_type=F32), a,
                precision=HI, preferred_element_type=F32,
            )
        a = 1.5 * eye - 0.5 * g
        move = jnp.dot(a, move, precision=HI, preferred_element_type=F32)
    mref[:, 0:32] = move

    land(srecv, pln, 9)
    land(xrecv, nx, 10)
    got = srecv[0].astype(F32)
    for w in range(1, pln):
        got = got + srecv[w].astype(F32)
    held = xrecv[lax.div(z, per)]
    held = jnp.concatenate([held, pltpu.roll(held, 64, 1)], axis=0)
    factor_ref[...] = jnp.dot(move, held[:, 0:64], precision=HI, preferred_element_type=F32)
    order = jnp.concatenate(
        [mref[pl.ds(0, 16, stride=2), :][:, 0:32], mref[pl.ds(1, 16, stride=2), :][:, 0:32]], axis=0
    )
    other = pltpu.roll(got, 64, 1)
    low16 = iota((16, 128), 1) < 64
    for t in range(2):
        both = jnp.where(low, got, other) if t == 0 else jnp.where(low, other, got)
        v = jnp.dot(order, both, precision=HI, preferred_element_type=F32)
        tf_ref[t] = jnp.where(low16, v[0:16], v[16:32]).astype(BF16)

    sent(tq, nz, 0)
    sent(req, pln, 1)
    sent(gbuf, pln, 2)
    sent(wrecv, pln, 3)
    sent(lrecv, nz, 4)
    sent(precv, pln, 5)
    sent(zrecv, pln, 6)
    sent(yrecv, nz, 7)
    pltpu.make_async_copy(part, part, send.at[11]).wait()
    sent(grecv, pln, 8)
    sent(srecv, pln, 9)
    sent(xrecv, nx, 10)
    sent(goes, pln, 12)


def solution(mesh):
    nx = mesh.shape["rep"]
    nz = mesh.shape["tiles"] // YC
    pln = nx * YC
    qr = 32 // nx
    per = nz // nx

    def per_device(tiles, block_one, block_two, block_three, owner_map, u_one, u_two, u_three):
        rows_total = owner_map.shape[0] * tiles.shape[1]
        vm = pl.BlockSpec(memory_space=pltpu.VMEM)
        factor, tf = pl.pallas_call(
            functools.partial(kernel, nx, nz, rows_total),
            out_shape=(
                jax.ShapeDtypeStruct((32, 64), F32),
                jax.ShapeDtypeStruct((2, 16, 128), BF16),
            ),
            in_specs=[pl.BlockSpec(memory_space=pltpu.HBM)] * 8,
            out_specs=(vm, vm),
            scratch_shapes=[
                pltpu.SMEM((2,), jnp.int32),
                pltpu.SMEM((2,), jnp.int32),
                pltpu.SMEM((2,), jnp.int32),
                pltpu.SMEM((owner_map.shape[0],), jnp.int32),
                pltpu.VMEM(u_one.shape, F32),
                pltpu.VMEM(u_two.shape, BF16),
                pltpu.VMEM(u_three.shape, BF16),
                pltpu.VMEM((128, 4096), BF16),
                pltpu.VMEM((32, 256), F32),
                pltpu.VMEM((qr, 256), BF16),
                pltpu.VMEM((nz, qr, 256), BF16),
                pltpu.VMEM((pln, 16, 384), BF16),
                pltpu.VMEM((16, 384), BF16),
                pltpu.VMEM((pln, 16, 128), BF16),
                pltpu.VMEM((pln, 16, 128), BF16),
                pltpu.VMEM((32, 64, 128), F32),
                pltpu.VMEM((1024, 128), BF16),
                pltpu.VMEM((pln, 8, 128), F32),
                pltpu.VMEM((pln, 8, 128), F32),
                pltpu.VMEM((8, 128), F32),
                pltpu.VMEM((nz, 8, 128), F32),
                pltpu.VMEM((8, 128), F32),
                pltpu.VMEM((pln, 8, 128), F32),
                pltpu.VMEM((32, 128), BF16),
                pltpu.VMEM((pln, 32, 128), BF16),
                pltpu.VMEM((8, 128), F32),
                pltpu.VMEM((pln, 8, 128), F32),
                pltpu.VMEM((32, per // 2, 128), F32),
                pltpu.VMEM((nz, 32 // nz, per // 2, 128), F32),
                pltpu.VMEM((32, per // 2, 128), F32),
                pltpu.VMEM((8, 128), F32),
                pltpu.VMEM((pln, 8, 128), F32),
                pltpu.VMEM((pln, 32, 128), BF16),
                pltpu.VMEM((pln, 32, 128), BF16),
                pltpu.VMEM((16, 128), F32),
                pltpu.VMEM((nx, 16, 128), F32),
                pltpu.VMEM((32, 128), F32),
                pltpu.SemaphoreType.DMA((9,)),
                pltpu.SemaphoreType.DMA((13,)),
                pltpu.SemaphoreType.DMA((13,)),
            ],
            compiler_params=pltpu.CompilerParams(
                collective_id=0, has_side_effects=True, vmem_limit_bytes=60 << 20
            ),
            name="hooi_step",
        )(tiles, block_one, block_two, block_three, owner_map, u_one, u_two, u_three)
        return factor, tf.reshape(2, 2048)

    in_specs = (
        P(("tiles", "rep"), None, None),
        P(("tiles", "rep")),
        P(("tiles", "rep")),
        P(("tiles", "rep")),
        P(),
        P(None, "tiles"),
        P(None, "tiles"),
        P(),
    )
    out_specs = (P(None, "tiles"), P(("tiles", "rep"), None))
    return jax.shard_map(
        per_device, mesh=mesh, in_specs=in_specs, out_specs=out_specs, check_vma=False
    )
```

```python
import functools

import jax
import jax.numpy as jnp
from jax import lax
from jax.experimental import pallas as pl
from jax.experimental.pallas import tpu as pltpu
from jax.sharding import PartitionSpec as P

MESH = pl.DeviceIdType.MESH
YC = 8
F32 = jnp.float32
BF16 = jnp.bfloat16
HI = lax.Precision.HIGHEST


def iota(shape, dim):
    return lax.broadcasted_iota(jnp.int32, shape, dim)


def nt(a, b, precision=None):
    return lax.dot_general(
        a, b, (((1,), (1,)), ((), ())), precision=precision, preferred_element_type=F32
    )


def kernel(
    nx, nz, rows_total,
    tiles_ref, b1_hbm, b2_hbm, b3_hbm, owner_hbm, u1_hbm, u2_hbm, u3_hbm,
    factor_ref, tf_ref,
    b1_ref, b2_ref, b3_ref, owner_ref, u1_ref, u2_ref, u3_ref,
    tl, us, shq, tq, req, reqs, obuf, gbuf, ft, pt, wsend, wrecv, lsend, lrecv, psend, precv,
    zsend, zrecv, gosend, goes, ysend, yrecv, yall, gsend, grecv, ssend, srecv, xsend, xrecv, mref,
    tsem, send, recv,
):
    pln = nx * YC
    per = nz // nx
    qr = 32 // nx
    t_id = lax.axis_index("tiles")
    x = lax.axis_index("rep")
    z = lax.div(t_id, YC)
    yc = lax.rem(t_id, YC)
    m = x * YC + yc

    copies = [
        pltpu.make_async_copy(tiles_ref.at[t], tl.at[pl.ds(64 * t, 64)], tsem.at[t])
        for t in range(2)
    ]
    inputs = [
        pltpu.make_async_copy(src, dst, tsem.at[2 + n])
        for n, (src, dst) in enumerate(
            ((u2_hbm, u2_ref), (u1_hbm, u1_ref), (b1_hbm, b1_ref), (owner_hbm, owner_ref),
             (b2_hbm, b2_ref), (b3_hbm, b3_ref), (u3_hbm, u3_ref))
        )
    ]

    def far(d, n):
        return min(d, n - d)

    xs = [lax.rem(x + d, nx) for d in range(nx)]
    ys = [lax.rem(lax.div(yc, 2) + d, YC // 2) * 2 for d in range(YC // 2)]
    cs = [lax.rem(yc, 2), 1 - lax.rem(yc, 2)]
    steps = [
        (far(dx, nx) + far(dy, YC // 2), dx, dy, dc)
        for dx in range(nx) for dy in range(YC // 2) for dc in range(2)
    ]
    steps = sorted(steps, reverse=True)[:-1]
    mates = [
        (xs[dx] * YC + ys[dy] + cs[dc], {"tiles": z * YC + ys[dy] + cs[dc], "rep": xs[dx]})
        for _, dx, dy, dc in steps
    ]
    zs = [lax.rem(z + d, nz) for d in sorted(range(1, nz), key=lambda d: -far(d, nz))]
    peers = [(w, {"tiles": w * YC + yc, "rep": x}) for w in zs]
    xmates = [(w, {"tiles": t_id, "rep": w}) for w in xs[1:]]

    barrier = pltpu.get_barrier_semaphore()
    for _, device in peers + mates:
        pl.semaphore_signal(barrier, inc=1, device_id=device, device_id_type=MESH)
    for c in inputs + copies:
        c.start()

    def post(who, phase, src, dst):
        for w, device in who:
            pltpu.make_async_remote_copy(
                src_ref=src(w), dst_ref=dst, send_sem=send.at[phase], recv_sem=recv.at[phase],
                device_id=device, device_id_type=MESH,
            ).start()

    def land(buf, n, phase):
        part = buf.at[pl.ds(0, n - 1)]
        pltpu.make_async_copy(part, part, recv.at[phase]).wait()

    def sent(buf, n, phase):
        part = buf.at[pl.ds(0, n - 1)]
        pltpu.make_async_copy(part, part, send.at[phase]).wait()

    for c in inputs[:2]:
        c.wait()
    us[:, pl.ds(0, 128)] = u2_ref[...].astype(F32)
    us[:, pl.ds(128, 64)] = jnp.zeros((32, 64), F32)
    us[:, pl.ds(192, 64)] = u1_ref[...]
    shq[...] = us[pl.ds(pl.multiple_of(x * qr, qr), qr), :].astype(BF16)
    pl.semaphore_wait(barrier, pln + nz - 2)
    post(peers, 0, lambda w: shq, tq.at[z])

    for c in inputs[2:]:
        c.wait()
    b2 = [b2_ref[t] for t in range(2)]
    b3 = [b3_ref[t] for t in range(2)]
    pos = [owner_ref[b1_ref[t]] for t in range(2)]

    r16 = iota((16, 128), 0)
    l16 = iota((16, 128), 1)

    def ask(q0, q1):
        want = jnp.where(r16 < qr, q0 * qr, q1 * qr - qr) + r16
        return jnp.where(l16 == want, 1.0, 0.0)

    ask_two = ask(lax.shift_right_logical(b2[0], 4), lax.shift_right_logical(b2[1], 4))
    odd = jnp.where(r16 < qr, lax.rem(b2[0], 2), lax.rem(b2[1], 2)) == 1
    reqs[:, 0:128] = jnp.where(odd, 0.0, ask_two).astype(BF16)
    reqs[:, 128:256] = jnp.where(odd, ask_two, 0.0).astype(BF16)
    reqs[:, 256:384] = ask(
        lax.shift_right_logical(pos[0], 3), lax.shift_right_logical(pos[1], 3)
    ).astype(BF16)
    post(mates, 1, lambda w: reqs, req.at[m])
    tq[z] = shq[...]
    req[m] = reqs[...]
    gosend[...] = jnp.where(iota((8, 128), 1) < 64, pos[0], pos[1]).astype(F32)
    goes[m] = gosend[...]

    lane128 = iota((32, 128), 1)
    spread = jnp.where(iota((256, 32), 0) // 8 == iota((256, 32), 1), 1.0, 0.0).astype(BF16)
    diag = []
    for t in range(2):
        chunk = jnp.zeros((32, 128), F32)
        for q in range(8):
            part = u3_ref[:, q * 128 : (q + 1) * 128].astype(F32)
            chunk = chunk + jnp.where(lax.shift_right_logical(b3[t], 1) == q, part, 0.0)
        swapped = pltpu.roll(chunk, 64, 1)
        odd = lax.rem(b3[t], 2) == 1
        twice = jnp.where((lane128 < 64) != odd, chunk, swapped)
        wide = jnp.dot(spread, twice.astype(BF16), preferred_element_type=F32)
        row = lax.rem(iota((256, 128), 0), 8)
        half = jnp.where(iota((256, 128), 1) < 64, 0, 1)
        diag.append(
            jnp.concatenate(
                [jnp.where(row == half + 2 * q, wide, 0.0).astype(BF16) for q in range(4)], axis=1
            )
        )
    for c in copies:
        c.wait()
    low256 = iota((256, 128), 1) < 64
    for jc in range(8):
        block = tl[:, jc * 512 : (jc + 1) * 512]
        out = jnp.where(low256, nt(diag[0], block), nt(diag[1], block))
        ft[:, jc * 8 : (jc + 1) * 8, :] = out.reshape(32, 8, 128)

    land(tq, nz, 0)
    land(req, pln, 1)
    table = tq[...].astype(F32).reshape(nz * qr, 256)
    halves = jnp.concatenate([table[:, 0:128], pltpu.roll(table[:, 0:128], 64, 1)], axis=0)
    two_part = jnp.dot(
        req[:, :, 0:256].reshape(pln * 16, 256), halves.astype(BF16), preferred_element_type=F32
    )
    one_part = jnp.dot(
        req[:, :, 256:384].reshape(pln * 16, 128), table[:, 128:256].astype(BF16),
        preferred_element_type=F32,
    )
    both = jnp.where(iota((pln * 16, 128), 1) < 64, two_part, one_part)
    obuf[...] = both.reshape(pln, 16, 128).astype(BF16)
    post(mates, 2, lambda w: obuf.at[w], gbuf.at[m])
    gbuf[m] = obuf[m]
    land(gbuf, pln, 2)

    held_two = [lax.rem(lax.shift_right_logical(b, 1), YC) for b in b2]
    held_one = [lax.rem(p, YC) for p in pos]
    holder = jnp.where(
        l16 < 64,
        jnp.where(r16 < 8, held_two[0], held_two[1]),
        jnp.where(r16 < 8, held_one[0], held_one[1]),
    )
    parts = []
    for xx in range(nx):
        acc = jnp.zeros((16, 128), F32)
        for cc in range(YC):
            acc = acc + jnp.where(holder == cc, gbuf[xx * YC + cc].astype(F32), 0.0)
        parts.append(acc)
    low = lane128 < 64
    picked = [jnp.concatenate([p[t * 8 : t * 8 + 8] for p in parts], axis=0) for t in range(2)]
    u2 = jnp.concatenate(picked, axis=0)[:, 0:64].astype(BF16)
    readers = jnp.where(low, pltpu.roll(picked[0], 64, 1), picked[1]).astype(BF16)

    for s in range(32):
        d = jnp.dot(u2, ft[s].astype(BF16), preferred_element_type=F32)
        pt[s * 32 : (s + 1) * 32, :] = jnp.where(low, d[0:32], d[32:64]).astype(BF16)

    w_part = nt(readers, pt[...])
    for q in range(8):
        wsend[:, q, :] = w_part[:, q * 128 : (q + 1) * 128]
    post(mates, 3, lambda w: wsend.at[w], wrecv.at[m])
    wrecv[m] = wsend[m]
    land(wrecv, pln, 3)
    lsend[...] = jnp.sum(wrecv[...], axis=0)
    post(peers, 4, lambda w: lsend, lrecv.at[z])
    lrecv[z] = lsend[...]
    post(mates, 12, lambda w: gosend, goes.at[m])
    land(lrecv, nz, 4)
    psend[...] = jnp.sum(lrecv[...], axis=0).astype(BF16).astype(F32)
    post(mates, 5, lambda w: psend, precv.at[m])
    precv[m] = psend[...]
    land(precv, pln, 5)
    project = jnp.concatenate([precv[:, q, :].astype(BF16) for q in range(8)], axis=1)

    zsend[...] = jnp.dot(project, pt[...], preferred_element_type=F32).astype(BF16)
    post(mates, 6, lambda w: zsend, zrecv.at[m])
    zrecv[m] = zsend[...]
    land(zrecv, pln, 6)
    mine = [((x * per + k) * YC + yc).astype(F32) for k in range(per)]
    land(goes, pln, 12)
    sums = [jnp.zeros((4, 8, 128), F32) for _ in range(per)]
    for w in range(pln):
        to = goes[w]
        val = zrecv[w].astype(F32).reshape(4, 8, 128)
        sums = [v + jnp.where((to == p)[None], val, 0.0) for v, p in zip(sums, mine)]
    sums = [v.reshape(32, 128) for v in sums]
    sums = [v + pltpu.roll(v, 64, 1) for v in sums]
    half = per // 2
    for h in range(half):
        ysend[:, h, :] = jnp.where(low, sums[2 * h], sums[2 * h + 1])
    rz = 32 // nz

    def slab(ref, w):
        return ref.at[pl.ds(w * rz, rz)]

    post(peers, 7, lambda w: slab(ysend, w), yrecv.at[z])
    yrecv[z] = ysend[pl.ds(z * rz, rz)]
    land(yrecv, nz, 7)
    yall[pl.ds(z * rz, rz)] = jnp.sum(yrecv[...], axis=0)
    post(peers, 11, lambda w: slab(yall, z), slab(yall, z))
    part = yall.at[pl.ds(0, rz * (nz - 1))]
    pltpu.make_async_copy(part, part, recv.at[11]).wait()
    total = jnp.concatenate([yall[:, h, :] for h in range(half)], axis=1)

    rounded = total.astype(BF16)
    gw = nt(rounded, jnp.concatenate([rounded] * 4, axis=0))
    lane8 = lax.shift_right_logical(iota((8, 128), 1), 5)
    packed = jnp.zeros((8, 128), F32)
    for q in range(4):
        packed = packed + jnp.where(lane8 == q, gw[q * 8 : q * 8 + 8], 0.0)
    gsend[...] = packed
    post(mates, 8, lambda w: gsend, grecv.at[m])
    grecv[m] = packed
    blocks = []
    for k in range(per):
        pair = total[:, (k // 2) * 128 : (k // 2) * 128 + 128]
        other = pltpu.roll(pair, 64, 1)
        blocks.append(jnp.where(low, pair, other) if k % 2 == 0 else jnp.where(low, other, pair))
    blocks = [v.reshape(4, 8, 128) for v in blocks]

    def answer(w):
        to = goes[w]
        val = jnp.zeros((4, 8, 128), F32)
        for v, p in zip(blocks, mine):
            val = val + jnp.where((to == p)[None], v, 0.0)
        return val.reshape(32, 128).astype(BF16)

    for w, device in mates:
        ssend[w] = answer(w)
        pltpu.make_async_remote_copy(
            src_ref=ssend.at[w], dst_ref=srecv.at[m], send_sem=send.at[9], recv_sem=recv.at[9],
            device_id=device, device_id_type=MESH,
        ).start()
    srecv[m] = answer(m)
    own = jnp.zeros((32, 128), F32)
    for k in range(per):
        own = own + jnp.where(lax.rem(z, per) == k, blocks[k].reshape(32, 128), 0.0)
    xsend[...] = jnp.where(low[0:16], own[0:16], own[16:32])
    post(xmates, 10, lambda w: xsend, xrecv.at[x])
    xrecv[x] = xsend[...]

    land(grecv, pln, 8)
    packed = jnp.sum(grecv[...], axis=0)
    tall = jnp.concatenate([jnp.where(lane8 == q, packed, 0.0) for q in range(4)], axis=0)
    fold = jnp.where(
        jnp.bitwise_and(iota((128, 32), 0), 31) == iota((128, 32), 1), 1.0, 0.0
    )
    g0 = jnp.dot(tall, fold, precision=HI, preferred_element_type=F32)
    eye = jnp.where(iota((32, 32), 0) == iota((32, 32), 1), 1.0, 0.0)
    trace = jnp.sum(jnp.sum(g0 * eye, axis=1, keepdims=True), axis=0, keepdims=True)
    inv = 1.0 / jnp.sqrt(trace / rows_total + 1e-06)
    g = g0 * (inv * inv) / rows_total
    a0 = 1.5 * eye - 0.5 * g
    g2 = jnp.dot(g, g, precision=HI, preferred_element_type=F32)
    a0a0 = 2.25 * eye - 1.5 * g + 0.25 * g2
    a0g = 1.5 * g - 0.5 * g2
    move = inv * (1.5 * a0 - 0.5 * jnp.dot(a0a0, a0g, precision=HI, preferred_element_type=F32))
    mref[:, 0:32] = move

    land(srecv, pln, 9)
    land(xrecv, nx, 10)
    got = srecv[0].astype(F32)
    for w in range(1, pln):
        got = got + srecv[w].astype(F32)
    held = xrecv[lax.div(z, per)]
    held = jnp.concatenate([held, pltpu.roll(held, 64, 1)], axis=0)
    factor_ref[...] = jnp.dot(move, held[:, 0:64], precision=HI, preferred_element_type=F32)
    order = jnp.concatenate(
        [mref[pl.ds(0, 16, stride=2), :][:, 0:32], mref[pl.ds(1, 16, stride=2), :][:, 0:32]], axis=0
    )
    other = pltpu.roll(got, 64, 1)
    low16 = iota((16, 128), 1) < 64
    for t in range(2):
        both = jnp.where(low, got, other) if t == 0 else jnp.where(low, other, got)
        v = jnp.dot(order, both, precision=HI, preferred_element_type=F32)
        tf_ref[t] = jnp.where(low16, v[0:16], v[16:32]).astype(BF16)

    sent(tq, nz, 0)
    sent(req, pln, 1)
    sent(gbuf, pln, 2)
    sent(wrecv, pln, 3)
    sent(lrecv, nz, 4)
    sent(precv, pln, 5)
    sent(zrecv, pln, 6)
    sent(yrecv, nz, 7)
    pltpu.make_async_copy(part, part, send.at[11]).wait()
    sent(grecv, pln, 8)
    sent(srecv, pln, 9)
    sent(xrecv, nx, 10)
    sent(goes, pln, 12)


def solution(mesh):
    nx = mesh.shape["rep"]
    nz = mesh.shape["tiles"] // YC
    pln = nx * YC
    qr = 32 // nx
    per = nz // nx

    def per_device(tiles, block_one, block_two, block_three, owner_map, u_one, u_two, u_three):
        rows_total = owner_map.shape[0] * tiles.shape[1]
        vm = pl.BlockSpec(memory_space=pltpu.VMEM)
        factor, tf = pl.pallas_call(
            functools.partial(kernel, nx, nz, rows_total),
            out_shape=(
                pltpu.VMEM((32, 64), F32),
                pltpu.VMEM((2, 16, 128), BF16),
            ),
            in_specs=[pl.BlockSpec(memory_space=pltpu.HBM)] * 8,
            out_specs=(vm, vm),
            scratch_shapes=[
                pltpu.SMEM((2,), jnp.int32),
                pltpu.SMEM((2,), jnp.int32),
                pltpu.SMEM((2,), jnp.int32),
                pltpu.SMEM((owner_map.shape[0],), jnp.int32),
                pltpu.VMEM(u_one.shape, F32),
                pltpu.VMEM(u_two.shape, BF16),
                pltpu.VMEM(u_three.shape, BF16),
                pltpu.VMEM((128, 4096), BF16),
                pltpu.VMEM((32, 256), F32),
                pltpu.VMEM((qr, 256), BF16),
                pltpu.VMEM((nz, qr, 256), BF16),
                pltpu.VMEM((pln, 16, 384), BF16),
                pltpu.VMEM((16, 384), BF16),
                pltpu.VMEM((pln, 16, 128), BF16),
                pltpu.VMEM((pln, 16, 128), BF16),
                pltpu.VMEM((32, 64, 128), F32),
                pltpu.VMEM((1024, 128), BF16),
                pltpu.VMEM((pln, 8, 128), F32),
                pltpu.VMEM((pln, 8, 128), F32),
                pltpu.VMEM((8, 128), F32),
                pltpu.VMEM((nz, 8, 128), F32),
                pltpu.VMEM((8, 128), F32),
                pltpu.VMEM((pln, 8, 128), F32),
                pltpu.VMEM((32, 128), BF16),
                pltpu.VMEM((pln, 32, 128), BF16),
                pltpu.VMEM((8, 128), F32),
                pltpu.VMEM((pln, 8, 128), F32),
                pltpu.VMEM((32, per // 2, 128), F32),
                pltpu.VMEM((nz, 32 // nz, per // 2, 128), F32),
                pltpu.VMEM((32, per // 2, 128), F32),
                pltpu.VMEM((8, 128), F32),
                pltpu.VMEM((pln, 8, 128), F32),
                pltpu.VMEM((pln, 32, 128), BF16),
                pltpu.VMEM((pln, 32, 128), BF16),
                pltpu.VMEM((16, 128), F32),
                pltpu.VMEM((nx, 16, 128), F32),
                pltpu.VMEM((32, 128), F32),
                pltpu.SemaphoreType.DMA((9,)),
                pltpu.SemaphoreType.DMA((13,)),
                pltpu.SemaphoreType.DMA((13,)),
            ],
            compiler_params=pltpu.CompilerParams(
                collective_id=0, has_side_effects=True, vmem_limit_bytes=60 << 20
            ),
            name="hooi_step",
        )(tiles, block_one, block_two, block_three, owner_map, u_one, u_two, u_three)
        return factor, tf.reshape(2, 2048)

    in_specs = (
        P(("tiles", "rep"), None, None),
        P(("tiles", "rep")),
        P(("tiles", "rep")),
        P(("tiles", "rep")),
        P(),
        P(None, "tiles"),
        P(None, "tiles"),
        P(),
    )
    out_specs = (P(None, "tiles"), P(("tiles", "rep"), None))
    return jax.shard_map(
        per_device, mesh=mesh, in_specs=in_specs, out_specs=out_specs, check_vma=False
    )
```

```python
import functools

import jax
import jax.numpy as jnp
from jax import lax
from jax.experimental import pallas as pl
from jax.experimental.pallas import tpu as pltpu
from jax.sharding import PartitionSpec as P

MESH = pl.DeviceIdType.MESH
YC = 8
F32 = jnp.float32
BF16 = jnp.bfloat16
HI = lax.Precision.HIGHEST


def iota(shape, dim):
    return lax.broadcasted_iota(jnp.int32, shape, dim)


def nt(a, b, precision=None):
    return lax.dot_general(
        a, b, (((1,), (1,)), ((), ())), precision=precision, preferred_element_type=F32
    )


def kernel(
    nx, nz, rows_total,
    tiles_ref, b1_hbm, b2_hbm, b3_hbm, owner_hbm, u1_hbm, u2_hbm, u3_hbm,
    factor_ref, tf_ref,
    b1_ref, b2_ref, b3_ref, owner_ref, u1_ref, u2_ref, u3_ref,
    tl, us, shq, tq, req, reqs, obuf, gbuf, ft, pt, wsend, whalf, wrecv, lsend, lrecv, psend, precv,
    zsend, zrecv, gosend, goes, ysend, yrecv, yall, gsend, grecv, ssend, srecv, xsend, xrecv, mref,
    tsem, send, recv,
):
    pln = nx * YC
    per = nz // nx
    qr = 32 // nx
    t_id = lax.axis_index("tiles")
    x = lax.axis_index("rep")
    z = lax.div(t_id, YC)
    yc = lax.rem(t_id, YC)
    m = x * YC + yc

    copies = [
        pltpu.make_async_copy(tiles_ref.at[t], tl.at[pl.ds(64 * t, 64)], tsem.at[t])
        for t in range(2)
    ]
    inputs = [
        pltpu.make_async_copy(src, dst, tsem.at[2 + n])
        for n, (src, dst) in enumerate(
            ((u2_hbm, u2_ref), (u1_hbm, u1_ref), (b1_hbm, b1_ref), (owner_hbm, owner_ref),
             (b2_hbm, b2_ref), (b3_hbm, b3_ref), (u3_hbm, u3_ref))
        )
    ]

    def far(d, n):
        return min(d, n - d)

    xs = [lax.rem(x + d, nx) for d in range(nx)]
    ys = [lax.rem(lax.div(yc, 2) + d, YC // 2) * 2 for d in range(YC // 2)]
    cs = [lax.rem(yc, 2), 1 - lax.rem(yc, 2)]
    steps = [
        (far(dx, nx) + far(dy, YC // 2), dx, dy, dc)
        for dx in range(nx) for dy in range(YC // 2) for dc in range(2)
    ]
    steps = sorted(steps, reverse=True)[:-1]
    mates = [
        (xs[dx] * YC + ys[dy] + cs[dc], {"tiles": z * YC + ys[dy] + cs[dc], "rep": xs[dx]})
        for _, dx, dy, dc in steps
    ]
    zs = [lax.rem(z + d, nz) for d in sorted(range(1, nz), key=lambda d: -far(d, nz))]
    peers = [(w, {"tiles": w * YC + yc, "rep": x}) for w in zs]
    xmates = [(w, {"tiles": t_id, "rep": w}) for w in xs[1:]]

    barrier = pltpu.get_barrier_semaphore()
    for _, device in peers + mates:
        pl.semaphore_signal(barrier, inc=1, device_id=device, device_id_type=MESH)
    for c in inputs + copies:
        c.start()

    def post(who, phase, src, dst):
        for w, device in who:
            pltpu.make_async_remote_copy(
                src_ref=src(w), dst_ref=dst, send_sem=send.at[phase], recv_sem=recv.at[phase],
                device_id=device, device_id_type=MESH,
            ).start()

    def land(buf, n, phase):
        part = buf.at[pl.ds(0, n - 1)]
        pltpu.make_async_copy(part, part, recv.at[phase]).wait()

    def sent(buf, n, phase):
        part = buf.at[pl.ds(0, n - 1)]
        pltpu.make_async_copy(part, part, send.at[phase]).wait()

    for c in inputs[:2]:
        c.wait()
    us[:, pl.ds(0, 128)] = u2_ref[...].astype(F32)
    us[:, pl.ds(128, 64)] = jnp.zeros((32, 64), F32)
    us[:, pl.ds(192, 64)] = u1_ref[...]
    shq[...] = us[pl.ds(pl.multiple_of(x * qr, qr), qr), :].astype(BF16)
    pl.semaphore_wait(barrier, pln + nz - 2)
    post(peers, 0, lambda w: shq, tq.at[z])

    for c in inputs[2:]:
        c.wait()
    b2 = [b2_ref[t] for t in range(2)]
    b3 = [b3_ref[t] for t in range(2)]
    pos = [owner_ref[b1_ref[t]] for t in range(2)]

    r16 = iota((16, 128), 0)
    l16 = iota((16, 128), 1)

    def ask(q0, q1):
        want = jnp.where(r16 < qr, q0 * qr, q1 * qr - qr) + r16
        return jnp.where(l16 == want, 1.0, 0.0)

    ask_two = ask(lax.shift_right_logical(b2[0], 4), lax.shift_right_logical(b2[1], 4))
    odd = jnp.where(r16 < qr, lax.rem(b2[0], 2), lax.rem(b2[1], 2)) == 1
    reqs[:, 0:128] = jnp.where(odd, 0.0, ask_two).astype(BF16)
    reqs[:, 128:256] = jnp.where(odd, ask_two, 0.0).astype(BF16)
    reqs[:, 256:384] = ask(
        lax.shift_right_logical(pos[0], 3), lax.shift_right_logical(pos[1], 3)
    ).astype(BF16)
    post(mates, 1, lambda w: reqs, req.at[m])
    tq[z] = shq[...]
    req[m] = reqs[...]
    gosend[...] = jnp.where(iota((8, 128), 1) < 64, pos[0], pos[1]).astype(F32)
    goes[m] = gosend[...]

    lane128 = iota((32, 128), 1)
    spread = jnp.where(iota((256, 32), 0) // 8 == iota((256, 32), 1), 1.0, 0.0).astype(BF16)
    diag = []
    for t in range(2):
        chunk = jnp.zeros((32, 128), F32)
        for q in range(8):
            part = u3_ref[:, q * 128 : (q + 1) * 128].astype(F32)
            chunk = chunk + jnp.where(lax.shift_right_logical(b3[t], 1) == q, part, 0.0)
        swapped = pltpu.roll(chunk, 64, 1)
        odd = lax.rem(b3[t], 2) == 1
        twice = jnp.where((lane128 < 64) != odd, chunk, swapped)
        wide = jnp.dot(spread, twice.astype(BF16), preferred_element_type=F32)
        row = lax.rem(iota((256, 128), 0), 8)
        half = jnp.where(iota((256, 128), 1) < 64, 0, 1)
        diag.append(
            jnp.concatenate(
                [jnp.where(row == half + 2 * q, wide, 0.0).astype(BF16) for q in range(4)], axis=1
            )
        )
    for c in copies:
        c.wait()
    low256 = iota((256, 128), 1) < 64
    for jc in range(8):
        block = tl[:, jc * 512 : (jc + 1) * 512]
        out = jnp.where(low256, nt(diag[0], block), nt(diag[1], block))
        ft[:, jc * 8 : (jc + 1) * 8, :] = out.reshape(32, 8, 128)

    land(tq, nz, 0)
    land(req, pln, 1)
    table = tq[...].astype(F32).reshape(nz * qr, 256)
    halves = jnp.concatenate([table[:, 0:128], pltpu.roll(table[:, 0:128], 64, 1)], axis=0)
    two_part = jnp.dot(
        req[:, :, 0:256].reshape(pln * 16, 256), halves.astype(BF16), preferred_element_type=F32
    )
    one_part = jnp.dot(
        req[:, :, 256:384].reshape(pln * 16, 128), table[:, 128:256].astype(BF16),
        preferred_element_type=F32,
    )
    both = jnp.where(iota((pln * 16, 128), 1) < 64, two_part, one_part)
    obuf[...] = both.reshape(pln, 16, 128).astype(BF16)
    post(mates, 2, lambda w: obuf.at[w], gbuf.at[m])
    gbuf[m] = obuf[m]
    land(gbuf, pln, 2)

    held_two = [lax.rem(lax.shift_right_logical(b, 1), YC) for b in b2]
    held_one = [lax.rem(p, YC) for p in pos]
    holder = jnp.where(
        l16 < 64,
        jnp.where(r16 < 8, held_two[0], held_two[1]),
        jnp.where(r16 < 8, held_one[0], held_one[1]),
    )
    parts = []
    for xx in range(nx):
        acc = jnp.zeros((16, 128), F32)
        for cc in range(YC):
            acc = acc + jnp.where(holder == cc, gbuf[xx * YC + cc].astype(F32), 0.0)
        parts.append(acc)
    low = lane128 < 64
    picked = [jnp.concatenate([p[t * 8 : t * 8 + 8] for p in parts], axis=0) for t in range(2)]
    u2 = jnp.concatenate(picked, axis=0)[:, 0:64].astype(BF16)
    readers = jnp.where(low, pltpu.roll(picked[0], 64, 1), picked[1]).astype(BF16)

    for s in range(32):
        d = jnp.dot(u2, ft[s].astype(BF16), preferred_element_type=F32)
        pt[s * 32 : (s + 1) * 32, :] = jnp.where(low, d[0:32], d[32:64]).astype(BF16)

    w_part = nt(readers, pt[...])
    for q in range(8):
        wsend[:, q, :] = w_part[:, q * 128 : (q + 1) * 128]
    whalf[...] = wsend[...].astype(BF16)
    post(mates, 3, lambda w: whalf.at[w], wrecv.at[m])
    wrecv[m] = whalf[m]
    land(wrecv, pln, 3)
    lsend[...] = jnp.sum(wrecv[...].astype(F32), axis=0).astype(BF16)
    post(peers, 4, lambda w: lsend, lrecv.at[z])
    lrecv[z] = lsend[...]
    post(mates, 12, lambda w: gosend, goes.at[m])
    land(lrecv, nz, 4)
    psend[...] = jnp.sum(lrecv[...].astype(F32), axis=0).astype(BF16)
    post(mates, 5, lambda w: psend, precv.at[m])
    precv[m] = psend[...]
    land(precv, pln, 5)
    wsend[...] = precv[...].astype(F32)
    project = jnp.concatenate([wsend[:, q, :].astype(BF16) for q in range(8)], axis=1)

    zsend[...] = jnp.dot(project, pt[...], preferred_element_type=F32).astype(BF16)
    post(mates, 6, lambda w: zsend, zrecv.at[m])
    zrecv[m] = zsend[...]
    land(zrecv, pln, 6)
    mine = [((x * per + k) * YC + yc).astype(F32) for k in range(per)]
    land(goes, pln, 12)
    sums = [jnp.zeros((4, 8, 128), F32) for _ in range(per)]
    for w in range(pln):
        to = goes[w]
        val = zrecv[w].astype(F32).reshape(4, 8, 128)
        sums = [v + jnp.where((to == p)[None], val, 0.0) for v, p in zip(sums, mine)]
    sums = [v.reshape(32, 128) for v in sums]
    sums = [v + pltpu.roll(v, 64, 1) for v in sums]
    half = per // 2
    for h in range(half):
        ysend[:, h, :] = jnp.where(low, sums[2 * h], sums[2 * h + 1])
    rz = 32 // nz

    def slab(ref, w):
        return ref.at[pl.ds(w * rz, rz)]

    post(peers, 7, lambda w: slab(ysend, w), yrecv.at[z])
    yrecv[z] = ysend[pl.ds(z * rz, rz)]
    land(yrecv, nz, 7)
    yall[pl.ds(z * rz, rz)] = jnp.sum(yrecv[...], axis=0)
    post(peers, 11, lambda w: slab(yall, z), slab(yall, z))
    part = yall.at[pl.ds(0, rz * (nz - 1))]
    pltpu.make_async_copy(part, part, recv.at[11]).wait()
    total = jnp.concatenate([yall[:, h, :] for h in range(half)], axis=1)

    rounded = total.astype(BF16)
    gw = nt(rounded, jnp.concatenate([rounded] * 4, axis=0))
    lane8 = lax.shift_right_logical(iota((8, 128), 1), 5)
    packed = jnp.zeros((8, 128), F32)
    for q in range(4):
        packed = packed + jnp.where(lane8 == q, gw[q * 8 : q * 8 + 8], 0.0)
    gsend[...] = packed
    post(mates, 8, lambda w: gsend, grecv.at[m])
    grecv[m] = packed
    blocks = []
    for k in range(per):
        pair = total[:, (k // 2) * 128 : (k // 2) * 128 + 128]
        other = pltpu.roll(pair, 64, 1)
        blocks.append(jnp.where(low, pair, other) if k % 2 == 0 else jnp.where(low, other, pair))
    blocks = [v.reshape(4, 8, 128) for v in blocks]

    def answer(w):
        to = goes[w]
        val = jnp.zeros((4, 8, 128), F32)
        for v, p in zip(blocks, mine):
            val = val + jnp.where((to == p)[None], v, 0.0)
        return val.reshape(32, 128).astype(BF16)

    for w, device in mates:
        ssend[w] = answer(w)
        pltpu.make_async_remote_copy(
            src_ref=ssend.at[w], dst_ref=srecv.at[m], send_sem=send.at[9], recv_sem=recv.at[9],
            device_id=device, device_id_type=MESH,
        ).start()
    srecv[m] = answer(m)
    own = jnp.zeros((32, 128), F32)
    for k in range(per):
        own = own + jnp.where(lax.rem(z, per) == k, blocks[k].reshape(32, 128), 0.0)
    xsend[...] = jnp.where(low[0:16], own[0:16], own[16:32])
    post(xmates, 10, lambda w: xsend, xrecv.at[x])
    xrecv[x] = xsend[...]

    land(grecv, pln, 8)
    packed = jnp.sum(grecv[...], axis=0)
    tall = jnp.concatenate([jnp.where(lane8 == q, packed, 0.0) for q in range(4)], axis=0)
    fold = jnp.where(
        jnp.bitwise_and(iota((128, 32), 0), 31) == iota((128, 32), 1), 1.0, 0.0
    )
    g0 = jnp.dot(tall, fold, precision=HI, preferred_element_type=F32)
    eye = jnp.where(iota((32, 32), 0) == iota((32, 32), 1), 1.0, 0.0)
    trace = jnp.sum(jnp.sum(g0 * eye, axis=1, keepdims=True), axis=0, keepdims=True)
    inv = 1.0 / jnp.sqrt(trace / rows_total + 1e-06)
    g = g0 * (inv * inv) / rows_total
    a0 = 1.5 * eye - 0.5 * g
    g2 = jnp.dot(g, g, precision=HI, preferred_element_type=F32)
    a0a0 = 2.25 * eye - 1.5 * g + 0.25 * g2
    a0g = 1.5 * g - 0.5 * g2
    move = inv * (1.5 * a0 - 0.5 * jnp.dot(a0a0, a0g, precision=HI, preferred_element_type=F32))
    mref[:, 0:32] = move

    land(srecv, pln, 9)
    land(xrecv, nx, 10)
    got = srecv[0].astype(F32)
    for w in range(1, pln):
        got = got + srecv[w].astype(F32)
    held = xrecv[lax.div(z, per)]
    held = jnp.concatenate([held, pltpu.roll(held, 64, 1)], axis=0)
    factor_ref[...] = jnp.dot(move, held[:, 0:64], precision=HI, preferred_element_type=F32)
    order = jnp.concatenate(
        [mref[pl.ds(0, 16, stride=2), :][:, 0:32], mref[pl.ds(1, 16, stride=2), :][:, 0:32]], axis=0
    )
    other = pltpu.roll(got, 64, 1)
    low16 = iota((16, 128), 1) < 64
    for t in range(2):
        both = jnp.where(low, got, other) if t == 0 else jnp.where(low, other, got)
        v = jnp.dot(order, both, precision=HI, preferred_element_type=F32)
        tf_ref[t] = jnp.where(low16, v[0:16], v[16:32]).astype(BF16)

    sent(tq, nz, 0)
    sent(req, pln, 1)
    sent(gbuf, pln, 2)
    sent(wrecv, pln, 3)
    sent(lrecv, nz, 4)
    sent(precv, pln, 5)
    sent(zrecv, pln, 6)
    sent(yrecv, nz, 7)
    pltpu.make_async_copy(part, part, send.at[11]).wait()
    sent(grecv, pln, 8)
    sent(srecv, pln, 9)
    sent(xrecv, nx, 10)
    sent(goes, pln, 12)


def solution(mesh):
    nx = mesh.shape["rep"]
    nz = mesh.shape["tiles"] // YC
    pln = nx * YC
    qr = 32 // nx
    per = nz // nx

    def per_device(tiles, block_one, block_two, block_three, owner_map, u_one, u_two, u_three):
        rows_total = owner_map.shape[0] * tiles.shape[1]
        vm = pl.BlockSpec(memory_space=pltpu.VMEM)
        factor, tf = pl.pallas_call(
            functools.partial(kernel, nx, nz, rows_total),
            out_shape=(
                pltpu.VMEM((32, 64), F32),
                pltpu.VMEM((2, 16, 128), BF16),
            ),
            in_specs=[pl.BlockSpec(memory_space=pltpu.HBM)] * 8,
            out_specs=(vm, vm),
            scratch_shapes=[
                pltpu.SMEM((2,), jnp.int32),
                pltpu.SMEM((2,), jnp.int32),
                pltpu.SMEM((2,), jnp.int32),
                pltpu.SMEM((owner_map.shape[0],), jnp.int32),
                pltpu.VMEM(u_one.shape, F32),
                pltpu.VMEM(u_two.shape, BF16),
                pltpu.VMEM(u_three.shape, BF16),
                pltpu.VMEM((128, 4096), BF16),
                pltpu.VMEM((32, 256), F32),
                pltpu.VMEM((qr, 256), BF16),
                pltpu.VMEM((nz, qr, 256), BF16),
                pltpu.VMEM((pln, 16, 384), BF16),
                pltpu.VMEM((16, 384), BF16),
                pltpu.VMEM((pln, 16, 128), BF16),
                pltpu.VMEM((pln, 16, 128), BF16),
                pltpu.VMEM((32, 64, 128), F32),
                pltpu.VMEM((1024, 128), BF16),
                pltpu.VMEM((pln, 8, 128), F32),
                pltpu.VMEM((pln, 8, 128), BF16),
                pltpu.VMEM((pln, 8, 128), BF16),
                pltpu.VMEM((8, 128), BF16),
                pltpu.VMEM((nz, 8, 128), BF16),
                pltpu.VMEM((8, 128), BF16),
                pltpu.VMEM((pln, 8, 128), BF16),
                pltpu.VMEM((32, 128), BF16),
                pltpu.VMEM((pln, 32, 128), BF16),
                pltpu.VMEM((8, 128), F32),
                pltpu.VMEM((pln, 8, 128), F32),
                pltpu.VMEM((32, per // 2, 128), F32),
                pltpu.VMEM((nz, 32 // nz, per // 2, 128), F32),
                pltpu.VMEM((32, per // 2, 128), F32),
                pltpu.VMEM((8, 128), F32),
                pltpu.VMEM((pln, 8, 128), F32),
                pltpu.VMEM((pln, 32, 128), BF16),
                pltpu.VMEM((pln, 32, 128), BF16),
                pltpu.VMEM((16, 128), F32),
                pltpu.VMEM((nx, 16, 128), F32),
                pltpu.VMEM((32, 128), F32),
                pltpu.SemaphoreType.DMA((9,)),
                pltpu.SemaphoreType.DMA((13,)),
                pltpu.SemaphoreType.DMA((13,)),
            ],
            compiler_params=pltpu.CompilerParams(
                collective_id=0, has_side_effects=True, vmem_limit_bytes=60 << 20
            ),
            name="hooi_step",
        )(tiles, block_one, block_two, block_three, owner_map, u_one, u_two, u_three)
        return factor, tf.reshape(2, 2048)

    in_specs = (
        P(("tiles", "rep"), None, None),
        P(("tiles", "rep")),
        P(("tiles", "rep")),
        P(("tiles", "rep")),
        P(),
        P(None, "tiles"),
        P(None, "tiles"),
        P(),
    )
    out_specs = (P(None, "tiles"), P(("tiles", "rep"), None))
    return jax.shard_map(
        per_device, mesh=mesh, in_specs=in_specs, out_specs=out_specs, check_vma=False
    )
```

```python
import functools

import jax
import jax.numpy as jnp
from jax import lax
from jax.experimental import pallas as pl
from jax.experimental.pallas import tpu as pltpu
from jax.sharding import PartitionSpec as P

MESH = pl.DeviceIdType.MESH
YC = 8
F32 = jnp.float32
BF16 = jnp.bfloat16
HI = lax.Precision.HIGHEST


def iota(shape, dim):
    return lax.broadcasted_iota(jnp.int32, shape, dim)


def nt(a, b, precision=None):
    return lax.dot_general(
        a, b, (((1,), (1,)), ((), ())), precision=precision, preferred_element_type=F32
    )


def kernel(
    nx, nz, rows_total,
    tiles_ref, b1_hbm, b2_hbm, b3_hbm, owner_hbm, u1_hbm, u2_hbm, u3_hbm,
    factor_ref, tf_ref,
    b1_ref, b2_ref, b3_ref, owner_ref, u1_ref, u2_ref, u3_ref,
    tl, us, shq, tq, req, reqs, obuf, gbuf, ft, pt, wsend, whalf, wrecv, lsend, lrecv, psend, precv,
    zsend, zrecv, gosend, goes, ysend, yrecv, yall, gsend, grecv, ssend, srecv, xsend, xrecv, mref,
    tsem, send, recv,
):
    pln = nx * YC
    per = nz // nx
    qr = 32 // nx
    t_id = lax.axis_index("tiles")
    x = lax.axis_index("rep")
    z = lax.div(t_id, YC)
    yc = lax.rem(t_id, YC)
    m = x * YC + yc

    copies = [
        pltpu.make_async_copy(tiles_ref.at[t], tl.at[pl.ds(64 * t, 64)], tsem.at[t])
        for t in range(2)
    ]
    inputs = [
        pltpu.make_async_copy(src, dst, tsem.at[2 + n])
        for n, (src, dst) in enumerate(
            ((u2_hbm, u2_ref), (u1_hbm, u1_ref), (b1_hbm, b1_ref), (owner_hbm, owner_ref),
             (b2_hbm, b2_ref), (b3_hbm, b3_ref), (u3_hbm, u3_ref))
        )
    ]

    def far(d, n):
        return min(d, n - d)

    xs = [lax.rem(x + d, nx) for d in range(nx)]
    ys = [lax.rem(lax.div(yc, 2) + d, YC // 2) * 2 for d in range(YC // 2)]
    cs = [lax.rem(yc, 2), 1 - lax.rem(yc, 2)]
    steps = [
        (far(dx, nx) + far(dy, YC // 2), dx, dy, dc)
        for dx in range(nx) for dy in range(YC // 2) for dc in range(2)
    ]
    steps = sorted(steps, reverse=True)[:-1]
    mates = [
        (xs[dx] * YC + ys[dy] + cs[dc], {"tiles": z * YC + ys[dy] + cs[dc], "rep": xs[dx]})
        for _, dx, dy, dc in steps
    ]
    zs = [lax.rem(z + d, nz) for d in sorted(range(1, nz), key=lambda d: -far(d, nz))]
    peers = [(w, {"tiles": w * YC + yc, "rep": x}) for w in zs]
    xmates = [(w, {"tiles": t_id, "rep": w}) for w in xs[1:]]

    near = nz // 4

    def along(d):
        return {"tiles": lax.rem(z + d + nz, nz) * YC + yc, "rep": x}

    close = [((nz - d) % nz, along(d)) for k in range(near, 0, -1) for d in (k, -k)]

    barrier = pltpu.get_barrier_semaphore()
    for _, device in close + mates:
        pl.semaphore_signal(barrier, inc=1, device_id=device, device_id_type=MESH)
    for c in inputs + copies:
        c.start()

    def post(who, phase, src, dst):
        for w, device in who:
            pltpu.make_async_remote_copy(
                src_ref=src(w), dst_ref=dst, send_sem=send.at[phase], recv_sem=recv.at[phase],
                device_id=device, device_id_type=MESH,
            ).start()

    def land(buf, n, phase):
        part = buf.at[pl.ds(0, n - 1)]
        pltpu.make_async_copy(part, part, recv.at[phase]).wait()

    def sent(buf, n, phase):
        part = buf.at[pl.ds(0, n - 1)]
        pltpu.make_async_copy(part, part, send.at[phase]).wait()

    for c in inputs[:2]:
        c.wait()
    us[:, pl.ds(0, 128)] = u2_ref[...].astype(F32)
    us[:, pl.ds(128, 64)] = jnp.zeros((32, 64), F32)
    us[:, pl.ds(192, 64)] = u1_ref[...]
    shq[...] = us[pl.ds(pl.multiple_of(x * qr, qr), qr), :].astype(BF16)
    pl.semaphore_wait(barrier, pln - 1 + 2 * near)
    for slot, device in close:
        pltpu.make_async_remote_copy(
            src_ref=shq, dst_ref=tq.at[slot], send_sem=send.at[0], recv_sem=recv.at[0],
            device_id=device, device_id_type=MESH,
        ).start()

    for c in inputs[2:]:
        c.wait()
    b2 = [b2_ref[t] for t in range(2)]
    b3 = [b3_ref[t] for t in range(2)]
    pos = [owner_ref[b1_ref[t]] for t in range(2)]

    r16 = iota((16, 128), 0)
    l16 = iota((16, 128), 1)

    def ask(q0, q1):
        want = jnp.where(r16 < qr, q0 * qr, q1 * qr - qr) + r16
        return jnp.where(l16 == want, 1.0, 0.0)

    def slot_of(at):
        return lax.rem(at - z + nz, nz)

    ask_two = ask(
        slot_of(lax.shift_right_logical(b2[0], 4)), slot_of(lax.shift_right_logical(b2[1], 4))
    )
    odd = jnp.where(r16 < qr, lax.rem(b2[0], 2), lax.rem(b2[1], 2)) == 1
    reqs[:, 0:128] = jnp.where(odd, 0.0, ask_two).astype(BF16)
    reqs[:, 128:256] = jnp.where(odd, ask_two, 0.0).astype(BF16)
    reqs[:, 256:384] = ask(
        slot_of(lax.shift_right_logical(pos[0], 3)), slot_of(lax.shift_right_logical(pos[1], 3))
    ).astype(BF16)
    post(mates, 1, lambda w: reqs, req.at[m])
    tq[0] = shq[...]
    req[m] = reqs[...]
    gosend[...] = jnp.where(iota((8, 128), 1) < 64, pos[0], pos[1]).astype(F32)
    goes[m] = gosend[...]

    lane128 = iota((32, 128), 1)
    spread = jnp.where(iota((256, 32), 0) // 8 == iota((256, 32), 1), 1.0, 0.0).astype(BF16)
    diag = []
    for t in range(2):
        chunk = jnp.zeros((32, 128), F32)
        for q in range(8):
            part = u3_ref[:, q * 128 : (q + 1) * 128].astype(F32)
            chunk = chunk + jnp.where(lax.shift_right_logical(b3[t], 1) == q, part, 0.0)
        swapped = pltpu.roll(chunk, 64, 1)
        odd = lax.rem(b3[t], 2) == 1
        twice = jnp.where((lane128 < 64) != odd, chunk, swapped)
        wide = jnp.dot(spread, twice.astype(BF16), preferred_element_type=F32)
        row = lax.rem(iota((256, 128), 0), 8)
        half = jnp.where(iota((256, 128), 1) < 64, 0, 1)
        diag.append(
            jnp.concatenate(
                [jnp.where(row == half + 2 * q, wide, 0.0).astype(BF16) for q in range(4)], axis=1
            )
        )
    for c in copies:
        c.wait()
    low256 = iota((256, 128), 1) < 64
    for jc in range(8):
        block = tl[:, jc * 512 : (jc + 1) * 512]
        out = jnp.where(low256, nt(diag[0], block), nt(diag[1], block))
        ft[:, jc * 8 : (jc + 1) * 8, :] = out.reshape(32, 8, 128)

    land(tq, 2 * near + 1, 0)
    for src, dst, count, d in ((1, near + 1, near, -near), (nz - near + 1, 2 * near + 1, near - 1, near)):
        pltpu.make_async_remote_copy(
            src_ref=tq.at[pl.ds(src, count)], dst_ref=tq.at[pl.ds(dst, count)],
            send_sem=send.at[13], recv_sem=recv.at[13],
            device_id=along(d), device_id_type=MESH,
        ).start()
    land(req, pln, 1)
    land(tq, 2 * near, 13)
    table = tq[...].astype(F32).reshape(nz * qr, 256)
    halves = jnp.concatenate([table[:, 0:128], pltpu.roll(table[:, 0:128], 64, 1)], axis=0)
    two_part = jnp.dot(
        req[:, :, 0:256].reshape(pln * 16, 256), halves.astype(BF16), preferred_element_type=F32
    )
    one_part = jnp.dot(
        req[:, :, 256:384].reshape(pln * 16, 128), table[:, 128:256].astype(BF16),
        preferred_element_type=F32,
    )
    both = jnp.where(iota((pln * 16, 128), 1) < 64, two_part, one_part)
    obuf[...] = both.reshape(pln, 16, 128).astype(BF16)
    post(mates, 2, lambda w: obuf.at[w], gbuf.at[m])
    gbuf[m] = obuf[m]
    land(gbuf, pln, 2)

    held_two = [lax.rem(lax.shift_right_logical(b, 1), YC) for b in b2]
    held_one = [lax.rem(p, YC) for p in pos]
    holder = jnp.where(
        l16 < 64,
        jnp.where(r16 < 8, held_two[0], held_two[1]),
        jnp.where(r16 < 8, held_one[0], held_one[1]),
    )
    parts = []
    for xx in range(nx):
        acc = jnp.zeros((16, 128), F32)
        for cc in range(YC):
            acc = acc + jnp.where(holder == cc, gbuf[xx * YC + cc].astype(F32), 0.0)
        parts.append(acc)
    low = lane128 < 64
    picked = [jnp.concatenate([p[t * 8 : t * 8 + 8] for p in parts], axis=0) for t in range(2)]
    u2 = jnp.concatenate(picked, axis=0)[:, 0:64].astype(BF16)
    readers = jnp.where(low, pltpu.roll(picked[0], 64, 1), picked[1]).astype(BF16)

    for s in range(32):
        d = jnp.dot(u2, ft[s].astype(BF16), preferred_element_type=F32)
        pt[s * 32 : (s + 1) * 32, :] = jnp.where(low, d[0:32], d[32:64]).astype(BF16)

    w_part = nt(readers, pt[...])
    for q in range(8):
        wsend[:, q, :] = w_part[:, q * 128 : (q + 1) * 128]
    whalf[...] = wsend[...].astype(BF16)
    post(mates, 3, lambda w: whalf.at[w], wrecv.at[m])
    wrecv[m] = whalf[m]
    land(wrecv, pln, 3)
    lsend[...] = jnp.sum(wrecv[...].astype(F32), axis=0).astype(BF16)
    post(peers, 4, lambda w: lsend, lrecv.at[z])
    lrecv[z] = lsend[...]
    post(mates, 12, lambda w: gosend, goes.at[m])
    land(lrecv, nz, 4)
    psend[...] = jnp.sum(lrecv[...].astype(F32), axis=0).astype(BF16)
    post(mates, 5, lambda w: psend, precv.at[m])
    precv[m] = psend[...]
    land(precv, pln, 5)
    wsend[...] = precv[...].astype(F32)
    project = jnp.concatenate([wsend[:, q, :].astype(BF16) for q in range(8)], axis=1)

    zsend[...] = jnp.dot(project, pt[...], preferred_element_type=F32).astype(BF16)
    post(mates, 6, lambda w: zsend, zrecv.at[m])
    zrecv[m] = zsend[...]
    land(zrecv, pln, 6)
    mine = [((x * per + k) * YC + yc).astype(F32) for k in range(per)]
    land(goes, pln, 12)
    sums = [jnp.zeros((4, 8, 128), F32) for _ in range(per)]
    for w in range(pln):
        to = goes[w]
        val = zrecv[w].astype(F32).reshape(4, 8, 128)
        sums = [v + jnp.where((to == p)[None], val, 0.0) for v, p in zip(sums, mine)]
    sums = [v.reshape(32, 128) for v in sums]
    sums = [v + pltpu.roll(v, 64, 1) for v in sums]
    half = per // 2
    for h in range(half):
        ysend[:, h, :] = jnp.where(low, sums[2 * h], sums[2 * h + 1])
    rz = 32 // nz

    def slab(ref, w):
        return ref.at[pl.ds(w * rz, rz)]

    post(peers, 7, lambda w: slab(ysend, w), yrecv.at[z])
    yrecv[z] = ysend[pl.ds(z * rz, rz)]
    land(yrecv, nz, 7)
    yall[pl.ds(z * rz, rz)] = jnp.sum(yrecv[...], axis=0)
    post(peers, 11, lambda w: slab(yall, z), slab(yall, z))
    part = yall.at[pl.ds(0, rz * (nz - 1))]
    pltpu.make_async_copy(part, part, recv.at[11]).wait()
    total = jnp.concatenate([yall[:, h, :] for h in range(half)], axis=1)

    rounded = total.astype(BF16)
    gw = nt(rounded, jnp.concatenate([rounded] * 4, axis=0))
    lane8 = lax.shift_right_logical(iota((8, 128), 1), 5)
    packed = jnp.zeros((8, 128), F32)
    for q in range(4):
        packed = packed + jnp.where(lane8 == q, gw[q * 8 : q * 8 + 8], 0.0)
    gsend[...] = packed
    post(mates, 8, lambda w: gsend, grecv.at[m])
    grecv[m] = packed
    blocks = []
    for k in range(per):
        pair = total[:, (k // 2) * 128 : (k // 2) * 128 + 128]
        other = pltpu.roll(pair, 64, 1)
        blocks.append(jnp.where(low, pair, other) if k % 2 == 0 else jnp.where(low, other, pair))
    blocks = [v.reshape(4, 8, 128) for v in blocks]

    def answer(w):
        to = goes[w]
        val = jnp.zeros((4, 8, 128), F32)
        for v, p in zip(blocks, mine):
            val = val + jnp.where((to == p)[None], v, 0.0)
        return val.reshape(32, 128).astype(BF16)

    for w, device in mates:
        ssend[w] = answer(w)
        pltpu.make_async_remote_copy(
            src_ref=ssend.at[w], dst_ref=srecv.at[m], send_sem=send.at[9], recv_sem=recv.at[9],
            device_id=device, device_id_type=MESH,
        ).start()
    srecv[m] = answer(m)
    own = jnp.zeros((32, 128), F32)
    for k in range(per):
        own = own + jnp.where(lax.rem(z, per) == k, blocks[k].reshape(32, 128), 0.0)
    xsend[...] = jnp.where(low[0:16], own[0:16], own[16:32])
    post(xmates, 10, lambda w: xsend, xrecv.at[x])
    xrecv[x] = xsend[...]

    land(grecv, pln, 8)
    packed = jnp.sum(grecv[...], axis=0)
    tall = jnp.concatenate([jnp.where(lane8 == q, packed, 0.0) for q in range(4)], axis=0)
    fold = jnp.where(
        jnp.bitwise_and(iota((128, 32), 0), 31) == iota((128, 32), 1), 1.0, 0.0
    )
    g0 = jnp.dot(tall, fold, precision=HI, preferred_element_type=F32)
    eye = jnp.where(iota((32, 32), 0) == iota((32, 32), 1), 1.0, 0.0)
    trace = jnp.sum(jnp.sum(g0 * eye, axis=1, keepdims=True), axis=0, keepdims=True)
    inv = 1.0 / jnp.sqrt(trace / rows_total + 1e-06)
    g = g0 * (inv * inv) / rows_total
    a0 = 1.5 * eye - 0.5 * g
    g2 = jnp.dot(g, g, precision=HI, preferred_element_type=F32)
    a0a0 = 2.25 * eye - 1.5 * g + 0.25 * g2
    a0g = 1.5 * g - 0.5 * g2
    move = inv * (1.5 * a0 - 0.5 * jnp.dot(a0a0, a0g, precision=HI, preferred_element_type=F32))
    mref[:, 0:32] = move

    land(srecv, pln, 9)
    land(xrecv, nx, 10)
    got = srecv[0].astype(F32)
    for w in range(1, pln):
        got = got + srecv[w].astype(F32)
    held = xrecv[lax.div(z, per)]
    held = jnp.concatenate([held, pltpu.roll(held, 64, 1)], axis=0)
    factor_ref[...] = jnp.dot(move, held[:, 0:64], precision=HI, preferred_element_type=F32)
    order = jnp.concatenate(
        [mref[pl.ds(0, 16, stride=2), :][:, 0:32], mref[pl.ds(1, 16, stride=2), :][:, 0:32]], axis=0
    )
    other = pltpu.roll(got, 64, 1)
    low16 = iota((16, 128), 1) < 64
    for t in range(2):
        both = jnp.where(low, got, other) if t == 0 else jnp.where(low, other, got)
        v = jnp.dot(order, both, precision=HI, preferred_element_type=F32)
        tf_ref[t] = jnp.where(low16, v[0:16], v[16:32]).astype(BF16)

    sent(tq, 2 * near + 1, 0)
    sent(tq, 2 * near, 13)
    sent(req, pln, 1)
    sent(gbuf, pln, 2)
    sent(wrecv, pln, 3)
    sent(lrecv, nz, 4)
    sent(precv, pln, 5)
    sent(zrecv, pln, 6)
    sent(yrecv, nz, 7)
    pltpu.make_async_copy(part, part, send.at[11]).wait()
    sent(grecv, pln, 8)
    sent(srecv, pln, 9)
    sent(xrecv, nx, 10)
    sent(goes, pln, 12)


def solution(mesh):
    nx = mesh.shape["rep"]
    nz = mesh.shape["tiles"] // YC
    pln = nx * YC
    qr = 32 // nx
    per = nz // nx

    def per_device(tiles, block_one, block_two, block_three, owner_map, u_one, u_two, u_three):
        rows_total = owner_map.shape[0] * tiles.shape[1]
        vm = pl.BlockSpec(memory_space=pltpu.VMEM)
        factor, tf = pl.pallas_call(
            functools.partial(kernel, nx, nz, rows_total),
            out_shape=(
                pltpu.VMEM((32, 64), F32),
                pltpu.VMEM((2, 16, 128), BF16),
            ),
            in_specs=[pl.BlockSpec(memory_space=pltpu.HBM)] * 8,
            out_specs=(vm, vm),
            scratch_shapes=[
                pltpu.SMEM((2,), jnp.int32),
                pltpu.SMEM((2,), jnp.int32),
                pltpu.SMEM((2,), jnp.int32),
                pltpu.SMEM((owner_map.shape[0],), jnp.int32),
                pltpu.VMEM(u_one.shape, F32),
                pltpu.VMEM(u_two.shape, BF16),
                pltpu.VMEM(u_three.shape, BF16),
                pltpu.VMEM((128, 4096), BF16),
                pltpu.VMEM((32, 256), F32),
                pltpu.VMEM((qr, 256), BF16),
                pltpu.VMEM((nz, qr, 256), BF16),
                pltpu.VMEM((pln, 16, 384), BF16),
                pltpu.VMEM((16, 384), BF16),
                pltpu.VMEM((pln, 16, 128), BF16),
                pltpu.VMEM((pln, 16, 128), BF16),
                pltpu.VMEM((32, 64, 128), F32),
                pltpu.VMEM((1024, 128), BF16),
                pltpu.VMEM((pln, 8, 128), F32),
                pltpu.VMEM((pln, 8, 128), BF16),
                pltpu.VMEM((pln, 8, 128), BF16),
                pltpu.VMEM((8, 128), BF16),
                pltpu.VMEM((nz, 8, 128), BF16),
                pltpu.VMEM((8, 128), BF16),
                pltpu.VMEM((pln, 8, 128), BF16),
                pltpu.VMEM((32, 128), BF16),
                pltpu.VMEM((pln, 32, 128), BF16),
                pltpu.VMEM((8, 128), F32),
                pltpu.VMEM((pln, 8, 128), F32),
                pltpu.VMEM((32, per // 2, 128), F32),
                pltpu.VMEM((nz, 32 // nz, per // 2, 128), F32),
                pltpu.VMEM((32, per // 2, 128), F32),
                pltpu.VMEM((8, 128), F32),
                pltpu.VMEM((pln, 8, 128), F32),
                pltpu.VMEM((pln, 32, 128), BF16),
                pltpu.VMEM((pln, 32, 128), BF16),
                pltpu.VMEM((16, 128), F32),
                pltpu.VMEM((nx, 16, 128), F32),
                pltpu.VMEM((32, 128), F32),
                pltpu.SemaphoreType.DMA((9,)),
                pltpu.SemaphoreType.DMA((14,)),
                pltpu.SemaphoreType.DMA((14,)),
            ],
            compiler_params=pltpu.CompilerParams(
                collective_id=0, has_side_effects=True, vmem_limit_bytes=60 << 20
            ),
            name="hooi_step",
        )(tiles, block_one, block_two, block_three, owner_map, u_one, u_two, u_three)
        return factor, tf.reshape(2, 2048)

    in_specs = (
        P(("tiles", "rep"), None, None),
        P(("tiles", "rep")),
        P(("tiles", "rep")),
        P(("tiles", "rep")),
        P(),
        P(None, "tiles"),
        P(None, "tiles"),
        P(),
    )
    out_specs = (P(None, "tiles"), P(("tiles", "rep"), None))
    return jax.shard_map(
        per_device, mesh=mesh, in_specs=in_specs, out_specs=out_specs, check_vma=False
    )
```

```python
import functools

import jax
import jax.numpy as jnp
from jax import lax
from jax.experimental import pallas as pl
from jax.experimental.pallas import tpu as pltpu
from jax.sharding import PartitionSpec as P

MESH = pl.DeviceIdType.MESH
YC = 8
F32 = jnp.float32
BF16 = jnp.bfloat16
HI = lax.Precision.HIGHEST


def iota(shape, dim):
    return lax.broadcasted_iota(jnp.int32, shape, dim)


def nt(a, b, precision=None):
    return lax.dot_general(
        a, b, (((1,), (1,)), ((), ())), precision=precision, preferred_element_type=F32
    )


def kernel(
    nx, nz, rows_total,
    tiles_ref, b1_hbm, b2_hbm, b3_hbm, owner_hbm, u1_hbm, u2_hbm, u3_hbm,
    factor_ref, tf_ref,
    b1_ref, b2_ref, b3_ref, owner_ref, u1_ref, u2_ref, u3_ref,
    tl, us, shq, tq, req, reqs, obuf, gbuf, ft, pt, wsend, whalf, wrecv, lsend, lrecv, psend, precv,
    zsend, zrecv, gosend, goes, ysend, yrecv, yall, gsend, grecv, ssend, srecv, xsend, xrecv, mref,
    tsem, send, recv,
):
    pln = nx * YC
    per = nz // nx
    qr = 32 // nx
    t_id = lax.axis_index("tiles")
    x = lax.axis_index("rep")
    z = lax.div(t_id, YC)
    yc = lax.rem(t_id, YC)
    m = x * YC + yc

    copies = [
        pltpu.make_async_copy(tiles_ref.at[t], tl.at[pl.ds(64 * t, 64)], tsem.at[t])
        for t in range(2)
    ]
    inputs = [
        pltpu.make_async_copy(src, dst, tsem.at[2 + n])
        for n, (src, dst) in enumerate(
            ((u2_hbm, u2_ref), (u1_hbm, u1_ref), (b1_hbm, b1_ref), (owner_hbm, owner_ref),
             (b2_hbm, b2_ref), (b3_hbm, b3_ref), (u3_hbm, u3_ref))
        )
    ]

    def far(d, n):
        return min(d, n - d)

    xs = [lax.rem(x + d, nx) for d in range(nx)]
    ys = [lax.rem(lax.div(yc, 2) + d, YC // 2) * 2 for d in range(YC // 2)]
    cs = [lax.rem(yc, 2), 1 - lax.rem(yc, 2)]
    steps = [
        (far(dx, nx) + far(dy, YC // 2), dx, dy, dc)
        for dx in range(nx) for dy in range(YC // 2) for dc in range(2)
    ]
    steps = sorted(steps, reverse=True)[:-1]
    mates = [
        (xs[dx] * YC + ys[dy] + cs[dc], {"tiles": z * YC + ys[dy] + cs[dc], "rep": xs[dx]})
        for _, dx, dy, dc in steps
    ]
    zs = [lax.rem(z + d, nz) for d in sorted(range(1, nz), key=lambda d: -far(d, nz))]
    peers = [(w, {"tiles": w * YC + yc, "rep": x}) for w in zs]
    xmates = [(w, {"tiles": t_id, "rep": w}) for w in xs[1:]]

    near = nz // 4

    def along(d):
        return {"tiles": lax.rem(z + d + nz, nz) * YC + yc, "rep": x}

    close = [((nz - d) % nz, along(d)) for k in range(near, 0, -1) for d in (k, -k)]

    barrier = pltpu.get_barrier_semaphore()
    for c in inputs[:2]:
        c.start()
    for _, device in close + mates:
        pl.semaphore_signal(barrier, inc=1, device_id=device, device_id_type=MESH)
    for c in inputs[2:] + copies:
        c.start()

    def post(who, phase, src, dst):
        for w, device in who:
            pltpu.make_async_remote_copy(
                src_ref=src(w), dst_ref=dst, send_sem=send.at[phase], recv_sem=recv.at[phase],
                device_id=device, device_id_type=MESH,
            ).start()

    def land(buf, n, phase):
        part = buf.at[pl.ds(0, n - 1)]
        pltpu.make_async_copy(part, part, recv.at[phase]).wait()

    def sent(buf, n, phase):
        part = buf.at[pl.ds(0, n - 1)]
        pltpu.make_async_copy(part, part, send.at[phase]).wait()

    for c in inputs[:2]:
        c.wait()
    us[:, pl.ds(0, 128)] = u2_ref[...].astype(F32)
    us[:, pl.ds(128, 64)] = jnp.zeros((32, 64), F32)
    us[:, pl.ds(192, 64)] = u1_ref[...]
    shq[...] = us[pl.ds(pl.multiple_of(x * qr, qr), qr), :].astype(BF16)
    pl.semaphore_wait(barrier, pln - 1 + 2 * near)
    for slot, device in close:
        pltpu.make_async_remote_copy(
            src_ref=shq, dst_ref=tq.at[slot], send_sem=send.at[0], recv_sem=recv.at[0],
            device_id=device, device_id_type=MESH,
        ).start()

    for c in inputs[2:]:
        c.wait()
    b2 = [b2_ref[t] for t in range(2)]
    b3 = [b3_ref[t] for t in range(2)]
    pos = [owner_ref[b1_ref[t]] for t in range(2)]

    r16 = iota((16, 128), 0)
    l16 = iota((16, 128), 1)

    def ask(q0, q1):
        want = jnp.where(r16 < qr, q0 * qr, q1 * qr - qr) + r16
        return jnp.where(l16 == want, 1.0, 0.0)

    def slot_of(at):
        return lax.rem(at - z + nz, nz)

    ask_two = ask(
        slot_of(lax.shift_right_logical(b2[0], 4)), slot_of(lax.shift_right_logical(b2[1], 4))
    )
    odd = jnp.where(r16 < qr, lax.rem(b2[0], 2), lax.rem(b2[1], 2)) == 1
    reqs[:, 0:128] = jnp.where(odd, 0.0, ask_two).astype(BF16)
    reqs[:, 128:256] = jnp.where(odd, ask_two, 0.0).astype(BF16)
    reqs[:, 256:384] = ask(
        slot_of(lax.shift_right_logical(pos[0], 3)), slot_of(lax.shift_right_logical(pos[1], 3))
    ).astype(BF16)
    post(mates, 1, lambda w: reqs, req.at[m])
    tq[0] = shq[...]
    req[m] = reqs[...]
    gosend[...] = jnp.where(iota((8, 128), 1) < 64, pos[0], pos[1]).astype(F32)
    goes[m] = gosend[...]

    lane128 = iota((32, 128), 1)
    spread = jnp.where(iota((256, 32), 0) // 8 == iota((256, 32), 1), 1.0, 0.0).astype(BF16)
    diag = []
    for t in range(2):
        chunk = jnp.zeros((32, 128), F32)
        for q in range(8):
            part = u3_ref[:, q * 128 : (q + 1) * 128].astype(F32)
            chunk = chunk + jnp.where(lax.shift_right_logical(b3[t], 1) == q, part, 0.0)
        swapped = pltpu.roll(chunk, 64, 1)
        odd = lax.rem(b3[t], 2) == 1
        twice = jnp.where((lane128 < 64) != odd, chunk, swapped)
        wide = jnp.dot(spread, twice.astype(BF16), preferred_element_type=F32)
        row = lax.rem(iota((256, 128), 0), 8)
        half = jnp.where(iota((256, 128), 1) < 64, 0, 1)
        diag.append(
            jnp.concatenate(
                [jnp.where(row == half + 2 * q, wide, 0.0).astype(BF16) for q in range(4)], axis=1
            )
        )
    for c in copies:
        c.wait()
    low256 = iota((256, 128), 1) < 64
    for jc in range(8):
        if jc == 4:
            land(tq, 2 * near + 1, 0)
            for src, dst, count, d in ((1, near + 1, near, -near), (nz - near + 1, 2 * near + 1, near - 1, near)):
                pltpu.make_async_remote_copy(
                    src_ref=tq.at[pl.ds(src, count)], dst_ref=tq.at[pl.ds(dst, count)],
                    send_sem=send.at[13], recv_sem=recv.at[13],
                    device_id=along(d), device_id_type=MESH,
                ).start()
        block = tl[:, jc * 512 : (jc + 1) * 512]
        out = jnp.where(low256, nt(diag[0], block), nt(diag[1], block))
        ft[:, jc * 8 : (jc + 1) * 8, :] = out.reshape(32, 8, 128)

    land(req, pln, 1)
    land(tq, 2 * near, 13)
    table = tq[...].astype(F32).reshape(nz * qr, 256)
    halves = jnp.concatenate([table[:, 0:128], pltpu.roll(table[:, 0:128], 64, 1)], axis=0)
    two_part = jnp.dot(
        req[:, :, 0:256].reshape(pln * 16, 256), halves.astype(BF16), preferred_element_type=F32
    )
    one_part = jnp.dot(
        req[:, :, 256:384].reshape(pln * 16, 128), table[:, 128:256].astype(BF16),
        preferred_element_type=F32,
    )
    both = jnp.where(iota((pln * 16, 128), 1) < 64, two_part, one_part)
    obuf[...] = both.reshape(pln, 16, 128).astype(BF16)
    post(mates, 2, lambda w: obuf.at[w], gbuf.at[m])
    gbuf[m] = obuf[m]
    land(gbuf, pln, 2)

    held_two = [lax.rem(lax.shift_right_logical(b, 1), YC) for b in b2]
    held_one = [lax.rem(p, YC) for p in pos]
    holder = jnp.where(
        l16 < 64,
        jnp.where(r16 < 8, held_two[0], held_two[1]),
        jnp.where(r16 < 8, held_one[0], held_one[1]),
    )
    parts = []
    for xx in range(nx):
        acc = jnp.zeros((16, 128), F32)
        for cc in range(YC):
            acc = acc + jnp.where(holder == cc, gbuf[xx * YC + cc].astype(F32), 0.0)
        parts.append(acc)
    low = lane128 < 64
    picked = [jnp.concatenate([p[t * 8 : t * 8 + 8] for p in parts], axis=0) for t in range(2)]
    u2 = jnp.concatenate(picked, axis=0)[:, 0:64].astype(BF16)
    readers = jnp.where(low, pltpu.roll(picked[0], 64, 1), picked[1]).astype(BF16)

    for s in range(32):
        d = jnp.dot(u2, ft[s].astype(BF16), preferred_element_type=F32)
        pt[s * 32 : (s + 1) * 32, :] = jnp.where(low, d[0:32], d[32:64]).astype(BF16)

    w_part = nt(readers, pt[...])
    for q in range(8):
        wsend[:, q, :] = w_part[:, q * 128 : (q + 1) * 128]
    whalf[...] = wsend[...].astype(BF16)
    post(mates, 3, lambda w: whalf.at[w], wrecv.at[m])
    wrecv[m] = whalf[m]
    land(wrecv, pln, 3)
    lsend[...] = jnp.sum(wrecv[...].astype(F32), axis=0).astype(BF16)
    post(peers, 4, lambda w: lsend, lrecv.at[z])
    lrecv[z] = lsend[...]
    post(mates, 12, lambda w: gosend, goes.at[m])
    land(lrecv, nz, 4)
    psend[...] = jnp.sum(lrecv[...].astype(F32), axis=0).astype(BF16)
    post(mates, 5, lambda w: psend, precv.at[m])
    precv[m] = psend[...]
    land(precv, pln, 5)
    wsend[...] = precv[...].astype(F32)
    project = jnp.concatenate([wsend[:, q, :].astype(BF16) for q in range(8)], axis=1)

    zsend[...] = jnp.dot(project, pt[...], preferred_element_type=F32).astype(BF16)
    post(mates, 6, lambda w: zsend, zrecv.at[m])
    zrecv[m] = zsend[...]
    land(zrecv, pln, 6)
    mine = [((x * per + k) * YC + yc).astype(F32) for k in range(per)]
    land(goes, pln, 12)
    sums = [jnp.zeros((4, 8, 128), F32) for _ in range(per)]
    for w in range(pln):
        to = goes[w]
        val = zrecv[w].astype(F32).reshape(4, 8, 128)
        sums = [v + jnp.where((to == p)[None], val, 0.0) for v, p in zip(sums, mine)]
    sums = [v.reshape(32, 128) for v in sums]
    sums = [v + pltpu.roll(v, 64, 1) for v in sums]
    half = per // 2
    for h in range(half):
        ysend[:, h, :] = jnp.where(low, sums[2 * h], sums[2 * h + 1])
    rz = 32 // nz

    def slab(ref, w):
        return ref.at[pl.ds(w * rz, rz)]

    post(peers, 7, lambda w: slab(ysend, w), yrecv.at[z])
    yrecv[z] = ysend[pl.ds(z * rz, rz)]
    land(yrecv, nz, 7)
    yall[pl.ds(z * rz, rz)] = jnp.sum(yrecv[...], axis=0)
    post(peers, 11, lambda w: slab(yall, z), slab(yall, z))
    part = yall.at[pl.ds(0, rz * (nz - 1))]
    pltpu.make_async_copy(part, part, recv.at[11]).wait()
    total = jnp.concatenate([yall[:, h, :] for h in range(half)], axis=1)

    rounded = total.astype(BF16)
    gw = nt(rounded, jnp.concatenate([rounded] * 4, axis=0))
    lane8 = lax.shift_right_logical(iota((8, 128), 1), 5)
    packed = jnp.zeros((8, 128), F32)
    for q in range(4):
        packed = packed + jnp.where(lane8 == q, gw[q * 8 : q * 8 + 8], 0.0)
    gsend[...] = packed
    post(mates, 8, lambda w: gsend, grecv.at[m])
    grecv[m] = packed
    blocks = []
    for k in range(per):
        pair = total[:, (k // 2) * 128 : (k // 2) * 128 + 128]
        other = pltpu.roll(pair, 64, 1)
        blocks.append(jnp.where(low, pair, other) if k % 2 == 0 else jnp.where(low, other, pair))
    blocks = [v.reshape(4, 8, 128) for v in blocks]

    def answer(w):
        to = goes[w]
        val = jnp.zeros((4, 8, 128), F32)
        for v, p in zip(blocks, mine):
            val = val + jnp.where((to == p)[None], v, 0.0)
        return val.reshape(32, 128).astype(BF16)

    for w, device in mates:
        ssend[w] = answer(w)
        pltpu.make_async_remote_copy(
            src_ref=ssend.at[w], dst_ref=srecv.at[m], send_sem=send.at[9], recv_sem=recv.at[9],
            device_id=device, device_id_type=MESH,
        ).start()
    srecv[m] = answer(m)
    own = jnp.zeros((32, 128), F32)
    for k in range(per):
        own = own + jnp.where(lax.rem(z, per) == k, blocks[k].reshape(32, 128), 0.0)
    xsend[...] = jnp.where(low[0:16], own[0:16], own[16:32])
    post(xmates, 10, lambda w: xsend, xrecv.at[x])
    xrecv[x] = xsend[...]

    land(grecv, pln, 8)
    packed = jnp.sum(grecv[...], axis=0)
    tall = jnp.concatenate([jnp.where(lane8 == q, packed, 0.0) for q in range(4)], axis=0)
    fold = jnp.where(
        jnp.bitwise_and(iota((128, 32), 0), 31) == iota((128, 32), 1), 1.0, 0.0
    )
    g0 = jnp.dot(tall, fold, precision=HI, preferred_element_type=F32)
    eye = jnp.where(iota((32, 32), 0) == iota((32, 32), 1), 1.0, 0.0)
    trace = jnp.sum(jnp.sum(g0 * eye, axis=1, keepdims=True), axis=0, keepdims=True)
    inv = 1.0 / jnp.sqrt(trace / rows_total + 1e-06)
    g = g0 * (inv * inv) / rows_total
    a0 = 1.5 * eye - 0.5 * g
    g2 = jnp.dot(g, g, precision=HI, preferred_element_type=F32)
    a0a0 = 2.25 * eye - 1.5 * g + 0.25 * g2
    a0g = 1.5 * g - 0.5 * g2
    move = inv * (1.5 * a0 - 0.5 * jnp.dot(a0a0, a0g, precision=HI, preferred_element_type=F32))
    mref[:, 0:32] = move

    land(srecv, pln, 9)
    land(xrecv, nx, 10)
    got = srecv[0].astype(F32)
    for w in range(1, pln):
        got = got + srecv[w].astype(F32)
    held = xrecv[lax.div(z, per)]
    held = jnp.concatenate([held, pltpu.roll(held, 64, 1)], axis=0)
    factor_ref[...] = jnp.dot(move, held[:, 0:64], precision=HI, preferred_element_type=F32)
    order = jnp.concatenate(
        [mref[pl.ds(0, 16, stride=2), :][:, 0:32], mref[pl.ds(1, 16, stride=2), :][:, 0:32]], axis=0
    )
    other = pltpu.roll(got, 64, 1)
    low16 = iota((16, 128), 1) < 64
    for t in range(2):
        both = jnp.where(low, got, other) if t == 0 else jnp.where(low, other, got)
        v = jnp.dot(order, both, precision=HI, preferred_element_type=F32)
        tf_ref[t] = jnp.where(low16, v[0:16], v[16:32]).astype(BF16)

    sent(tq, 2 * near + 1, 0)
    sent(tq, 2 * near, 13)
    sent(req, pln, 1)
    sent(gbuf, pln, 2)
    sent(wrecv, pln, 3)
    sent(lrecv, nz, 4)
    sent(precv, pln, 5)
    sent(zrecv, pln, 6)
    sent(yrecv, nz, 7)
    pltpu.make_async_copy(part, part, send.at[11]).wait()
    sent(grecv, pln, 8)
    sent(srecv, pln, 9)
    sent(xrecv, nx, 10)
    sent(goes, pln, 12)


def solution(mesh):
    nx = mesh.shape["rep"]
    nz = mesh.shape["tiles"] // YC
    pln = nx * YC
    qr = 32 // nx
    per = nz // nx

    def per_device(tiles, block_one, block_two, block_three, owner_map, u_one, u_two, u_three):
        rows_total = owner_map.shape[0] * tiles.shape[1]
        vm = pl.BlockSpec(memory_space=pltpu.VMEM)
        factor, tf = pl.pallas_call(
            functools.partial(kernel, nx, nz, rows_total),
            out_shape=(
                pltpu.VMEM((32, 64), F32),
                pltpu.VMEM((2, 16, 128), BF16),
            ),
            in_specs=[pl.BlockSpec(memory_space=pltpu.HBM)] * 8,
            out_specs=(vm, vm),
            scratch_shapes=[
                pltpu.SMEM((2,), jnp.int32),
                pltpu.SMEM((2,), jnp.int32),
                pltpu.SMEM((2,), jnp.int32),
                pltpu.SMEM((owner_map.shape[0],), jnp.int32),
                pltpu.VMEM(u_one.shape, F32),
                pltpu.VMEM(u_two.shape, BF16),
                pltpu.VMEM(u_three.shape, BF16),
                pltpu.VMEM((128, 4096), BF16),
                pltpu.VMEM((32, 256), F32),
                pltpu.VMEM((qr, 256), BF16),
                pltpu.VMEM((nz, qr, 256), BF16),
                pltpu.VMEM((pln, 16, 384), BF16),
                pltpu.VMEM((16, 384), BF16),
                pltpu.VMEM((pln, 16, 128), BF16),
                pltpu.VMEM((pln, 16, 128), BF16),
                pltpu.VMEM((32, 64, 128), F32),
                pltpu.VMEM((1024, 128), BF16),
                pltpu.VMEM((pln, 8, 128), F32),
                pltpu.VMEM((pln, 8, 128), BF16),
                pltpu.VMEM((pln, 8, 128), BF16),
                pltpu.VMEM((8, 128), BF16),
                pltpu.VMEM((nz, 8, 128), BF16),
                pltpu.VMEM((8, 128), BF16),
                pltpu.VMEM((pln, 8, 128), BF16),
                pltpu.VMEM((32, 128), BF16),
                pltpu.VMEM((pln, 32, 128), BF16),
                pltpu.VMEM((8, 128), F32),
                pltpu.VMEM((pln, 8, 128), F32),
                pltpu.VMEM((32, per // 2, 128), F32),
                pltpu.VMEM((nz, 32 // nz, per // 2, 128), F32),
                pltpu.VMEM((32, per // 2, 128), F32),
                pltpu.VMEM((8, 128), F32),
                pltpu.VMEM((pln, 8, 128), F32),
                pltpu.VMEM((pln, 32, 128), BF16),
                pltpu.VMEM((pln, 32, 128), BF16),
                pltpu.VMEM((16, 128), F32),
                pltpu.VMEM((nx, 16, 128), F32),
                pltpu.VMEM((32, 128), F32),
                pltpu.SemaphoreType.DMA((9,)),
                pltpu.SemaphoreType.DMA((14,)),
                pltpu.SemaphoreType.DMA((14,)),
            ],
            compiler_params=pltpu.CompilerParams(
                collective_id=0, has_side_effects=True, vmem_limit_bytes=60 << 20
            ),
            name="hooi_step",
        )(tiles, block_one, block_two, block_three, owner_map, u_one, u_two, u_three)
        return factor, tf.reshape(2, 2048)

    in_specs = (
        P(("tiles", "rep"), None, None),
        P(("tiles", "rep")),
        P(("tiles", "rep")),
        P(("tiles", "rep")),
        P(),
        P(None, "tiles"),
        P(None, "tiles"),
        P(),
    )
    out_specs = (P(None, "tiles"), P(("tiles", "rep"), None))
    return jax.shard_map(
        per_device, mesh=mesh, in_specs=in_specs, out_specs=out_specs, check_vma=False
    )
```

```python
import functools

import jax
import jax.numpy as jnp
from jax import lax
from jax.experimental import pallas as pl
from jax.experimental.pallas import tpu as pltpu
from jax.sharding import PartitionSpec as P

MESH = pl.DeviceIdType.MESH
YC = 8
F32 = jnp.float32
BF16 = jnp.bfloat16
HI = lax.Precision.HIGHEST


def iota(shape, dim):
    return lax.broadcasted_iota(jnp.int32, shape, dim)


def nt(a, b, precision=None):
    return lax.dot_general(
        a, b, (((1,), (1,)), ((), ())), precision=precision, preferred_element_type=F32
    )


def kernel(
    nx, nz, rows_total,
    tiles_ref, b1_hbm, b2_hbm, b3_hbm, owner_hbm, u1_hbm, u2_hbm, u3_hbm,
    factor_ref, tf_ref,
    b1_ref, b2_ref, b3_ref, owner_ref, u1_ref, u2_ref, u3_ref,
    tl, us, shq, tq, req, reqs, obuf, gbuf, ft, pt, wsend, whalf, wrecv, lsend, lrecv, psend, precv,
    zsend, zrecv, gosend, goes, ysend, yrecv, yall, gsend, grecv, ssend, srecv, xsend, xrecv, mref,
    tsem, send, recv,
):
    pln = nx * YC
    per = nz // nx
    qr = 32 // nx
    t_id = lax.axis_index("tiles")
    x = lax.axis_index("rep")
    z = lax.div(t_id, YC)
    yc = lax.rem(t_id, YC)
    m = x * YC + yc

    copies = [
        pltpu.make_async_copy(tiles_ref.at[t], tl.at[pl.ds(64 * t, 64)], tsem.at[t])
        for t in range(2)
    ]
    inputs = [
        pltpu.make_async_copy(src, dst, tsem.at[2 + n])
        for n, (src, dst) in enumerate(
            ((u2_hbm, u2_ref), (u1_hbm, u1_ref), (b1_hbm, b1_ref), (owner_hbm, owner_ref),
             (b2_hbm, b2_ref), (b3_hbm, b3_ref), (u3_hbm, u3_ref))
        )
    ]

    def far(d, n):
        return min(d, n - d)

    xs = [lax.rem(x + d, nx) for d in range(nx)]
    ys = [lax.rem(lax.div(yc, 2) + d, YC // 2) * 2 for d in range(YC // 2)]
    cs = [lax.rem(yc, 2), 1 - lax.rem(yc, 2)]
    steps = [
        (far(dx, nx) + far(dy, YC // 2), dx, dy, dc)
        for dx in range(nx) for dy in range(YC // 2) for dc in range(2)
    ]
    steps = sorted(steps, reverse=True)[:-1]
    mates = [
        (xs[dx] * YC + ys[dy] + cs[dc], {"tiles": z * YC + ys[dy] + cs[dc], "rep": xs[dx]})
        for _, dx, dy, dc in steps
    ]
    zs = [lax.rem(z + d, nz) for d in sorted(range(1, nz), key=lambda d: -far(d, nz))]
    peers = [(w, {"tiles": w * YC + yc, "rep": x}) for w in zs]
    xmates = [(w, {"tiles": t_id, "rep": w}) for w in xs[1:]]

    near = nz // 4

    def along(d):
        return {"tiles": lax.rem(z + d + nz, nz) * YC + yc, "rep": x}

    close = [((nz - d) % nz, along(d)) for k in range(near, 0, -1) for d in (k, -k)]

    barrier = pltpu.get_barrier_semaphore()
    for c in inputs[:2]:
        c.start()
    for _, device in close + mates:
        pl.semaphore_signal(barrier, inc=1, device_id=device, device_id_type=MESH)
    for c in inputs[2:] + copies:
        c.start()

    def post(who, phase, src, dst):
        for w, device in who:
            pltpu.make_async_remote_copy(
                src_ref=src(w), dst_ref=dst, send_sem=send.at[phase], recv_sem=recv.at[phase],
                device_id=device, device_id_type=MESH,
            ).start()

    def land(buf, n, phase):
        part = buf.at[pl.ds(0, n - 1)]
        pltpu.make_async_copy(part, part, recv.at[phase]).wait()

    def sent(buf, n, phase):
        part = buf.at[pl.ds(0, n - 1)]
        pltpu.make_async_copy(part, part, send.at[phase]).wait()

    for c in inputs[:2]:
        c.wait()
    us[:, pl.ds(0, 128)] = u2_ref[...].astype(F32)
    us[:, pl.ds(128, 64)] = jnp.zeros((32, 64), F32)
    us[:, pl.ds(192, 64)] = u1_ref[...]
    shq[...] = us[pl.ds(pl.multiple_of(x * qr, qr), qr), :].astype(BF16)
    pl.semaphore_wait(barrier, pln - 1 + 2 * near)
    for slot, device in close:
        pltpu.make_async_remote_copy(
            src_ref=shq, dst_ref=tq.at[slot], send_sem=send.at[0], recv_sem=recv.at[0],
            device_id=device, device_id_type=MESH,
        ).start()

    for c in inputs[2:]:
        c.wait()
    b2 = [b2_ref[t] for t in range(2)]
    b3 = [b3_ref[t] for t in range(2)]
    pos = [owner_ref[b1_ref[t]] for t in range(2)]

    r16 = iota((16, 128), 0)
    l16 = iota((16, 128), 1)

    def ask(q0, q1):
        want = jnp.where(r16 < qr, q0 * qr, q1 * qr - qr) + r16
        return jnp.where(l16 == want, 1.0, 0.0)

    def slot_of(at):
        return lax.rem(at - z + nz, nz)

    ask_two = ask(
        slot_of(lax.shift_right_logical(b2[0], 4)), slot_of(lax.shift_right_logical(b2[1], 4))
    )
    odd = jnp.where(r16 < qr, lax.rem(b2[0], 2), lax.rem(b2[1], 2)) == 1
    reqs[:, 0:128] = jnp.where(odd, 0.0, ask_two).astype(BF16)
    reqs[:, 128:256] = jnp.where(odd, ask_two, 0.0).astype(BF16)
    reqs[:, 256:384] = ask(
        slot_of(lax.shift_right_logical(pos[0], 3)), slot_of(lax.shift_right_logical(pos[1], 3))
    ).astype(BF16)
    post(mates, 1, lambda w: reqs, req.at[m])
    tq[0] = shq[...]
    req[m] = reqs[...]
    gosend[...] = jnp.where(iota((8, 128), 1) < 64, pos[0], pos[1]).astype(F32)
    goes[m] = gosend[...]
    post(mates, 12, lambda w: gosend, goes.at[m])

    lane128 = iota((32, 128), 1)
    spread = jnp.where(iota((256, 32), 0) // 8 == iota((256, 32), 1), 1.0, 0.0).astype(BF16)
    diag = []
    for t in range(2):
        chunk = jnp.zeros((32, 128), F32)
        for q in range(8):
            part = u3_ref[:, q * 128 : (q + 1) * 128].astype(F32)
            chunk = chunk + jnp.where(lax.shift_right_logical(b3[t], 1) == q, part, 0.0)
        swapped = pltpu.roll(chunk, 64, 1)
        odd = lax.rem(b3[t], 2) == 1
        twice = jnp.where((lane128 < 64) != odd, chunk, swapped)
        wide = jnp.dot(spread, twice.astype(BF16), preferred_element_type=F32)
        row = lax.rem(iota((256, 128), 0), 8)
        half = jnp.where(iota((256, 128), 1) < 64, 0, 1)
        diag.append(
            jnp.concatenate(
                [jnp.where(row == half + 2 * q, wide, 0.0).astype(BF16) for q in range(4)], axis=1
            )
        )
    for c in copies:
        c.wait()
    low256 = iota((256, 128), 1) < 64
    for jc in range(8):
        if jc == 4:
            land(tq, 2 * near + 1, 0)
            for src, dst, count, d in ((1, near + 1, near, -near), (nz - near + 1, 2 * near + 1, near - 1, near)):
                pltpu.make_async_remote_copy(
                    src_ref=tq.at[pl.ds(src, count)], dst_ref=tq.at[pl.ds(dst, count)],
                    send_sem=send.at[13], recv_sem=recv.at[13],
                    device_id=along(d), device_id_type=MESH,
                ).start()
        block = tl[:, jc * 512 : (jc + 1) * 512]
        out = jnp.where(low256, nt(diag[0], block), nt(diag[1], block))
        ft[:, jc * 8 : (jc + 1) * 8, :] = out.reshape(32, 8, 128)

    land(req, pln, 1)
    land(tq, 2 * near, 13)
    table = tq[...].astype(F32).reshape(nz * qr, 256)
    halves = jnp.concatenate([table[:, 0:128], pltpu.roll(table[:, 0:128], 64, 1)], axis=0)
    two_part = jnp.dot(
        req[:, :, 0:256].reshape(pln * 16, 256), halves.astype(BF16), preferred_element_type=F32
    )
    one_part = jnp.dot(
        req[:, :, 256:384].reshape(pln * 16, 128), table[:, 128:256].astype(BF16),
        preferred_element_type=F32,
    )
    both = jnp.where(iota((pln * 16, 128), 1) < 64, two_part, one_part)
    obuf[...] = both.reshape(pln, 16, 128).astype(BF16)
    post(mates, 2, lambda w: obuf.at[w], gbuf.at[m])
    gbuf[m] = obuf[m]
    land(gbuf, pln, 2)

    held_two = [lax.rem(lax.shift_right_logical(b, 1), YC) for b in b2]
    held_one = [lax.rem(p, YC) for p in pos]
    holder = jnp.where(
        l16 < 64,
        jnp.where(r16 < 8, held_two[0], held_two[1]),
        jnp.where(r16 < 8, held_one[0], held_one[1]),
    )
    parts = []
    for xx in range(nx):
        acc = jnp.zeros((16, 128), F32)
        for cc in range(YC):
            acc = acc + jnp.where(holder == cc, gbuf[xx * YC + cc].astype(F32), 0.0)
        parts.append(acc)
    low = lane128 < 64
    picked = [jnp.concatenate([p[t * 8 : t * 8 + 8] for p in parts], axis=0) for t in range(2)]
    u2 = jnp.concatenate(picked, axis=0)[:, 0:64].astype(BF16)
    readers = jnp.where(low, pltpu.roll(picked[0], 64, 1), picked[1]).astype(BF16)

    for s in range(32):
        d = jnp.dot(u2, ft[s].astype(BF16), preferred_element_type=F32)
        pt[s * 32 : (s + 1) * 32, :] = jnp.where(low, d[0:32], d[32:64]).astype(BF16)

    w_part = nt(readers, pt[...])
    for q in range(8):
        wsend[:, q, :] = w_part[:, q * 128 : (q + 1) * 128]
    whalf[...] = wsend[...].astype(BF16)
    post(mates, 3, lambda w: whalf.at[w], wrecv.at[m])
    wrecv[m] = whalf[m]
    land(wrecv, pln, 3)
    lsend[...] = jnp.sum(wrecv[...].astype(F32), axis=0).astype(BF16)
    post(peers, 4, lambda w: lsend, lrecv.at[z])
    lrecv[z] = lsend[...]
    land(lrecv, nz, 4)
    psend[...] = jnp.sum(lrecv[...].astype(F32), axis=0).astype(BF16)
    post(mates, 5, lambda w: psend, precv.at[m])
    precv[m] = psend[...]
    land(precv, pln, 5)
    wsend[...] = precv[...].astype(F32)
    project = jnp.concatenate([wsend[:, q, :].astype(BF16) for q in range(8)], axis=1)

    zsend[...] = jnp.dot(project, pt[...], preferred_element_type=F32).astype(BF16)
    post(mates, 6, lambda w: zsend, zrecv.at[m])
    zrecv[m] = zsend[...]
    land(zrecv, pln, 6)
    mine = [((x * per + k) * YC + yc).astype(F32) for k in range(per)]
    land(goes, pln, 12)
    sums = [jnp.zeros((4, 8, 128), F32) for _ in range(per)]
    for w in range(pln):
        to = goes[w]
        val = zrecv[w].astype(F32).reshape(4, 8, 128)
        sums = [v + jnp.where((to == p)[None], val, 0.0) for v, p in zip(sums, mine)]
    sums = [v.reshape(32, 128) for v in sums]
    sums = [v + pltpu.roll(v, 64, 1) for v in sums]
    half = per // 2
    for h in range(half):
        ysend[:, h, :] = jnp.where(low, sums[2 * h], sums[2 * h + 1])
    rz = 32 // nz

    def slab(ref, w):
        return ref.at[pl.ds(w * rz, rz)]

    post(peers, 7, lambda w: slab(ysend, w), yrecv.at[z])
    yrecv[z] = ysend[pl.ds(z * rz, rz)]
    land(yrecv, nz, 7)
    yall[pl.ds(z * rz, rz)] = jnp.sum(yrecv[...], axis=0)
    post(peers, 11, lambda w: slab(yall, z), slab(yall, z))
    part = yall.at[pl.ds(0, rz * (nz - 1))]
    pltpu.make_async_copy(part, part, recv.at[11]).wait()
    total = jnp.concatenate([yall[:, h, :] for h in range(half)], axis=1)

    rounded = total.astype(BF16)
    gw = nt(rounded, jnp.concatenate([rounded] * 4, axis=0))
    lane8 = lax.shift_right_logical(iota((8, 128), 1), 5)
    packed = jnp.zeros((8, 128), F32)
    for q in range(4):
        packed = packed + jnp.where(lane8 == q, gw[q * 8 : q * 8 + 8], 0.0)
    gsend[...] = packed
    post(mates, 8, lambda w: gsend, grecv.at[m])
    grecv[m] = packed
    blocks = []
    for k in range(per):
        pair = total[:, (k // 2) * 128 : (k // 2) * 128 + 128]
        other = pltpu.roll(pair, 64, 1)
        blocks.append(jnp.where(low, pair, other) if k % 2 == 0 else jnp.where(low, other, pair))
    blocks = [v.reshape(4, 8, 128) for v in blocks]

    def answer(w):
        to = goes[w]
        val = jnp.zeros((4, 8, 128), F32)
        for v, p in zip(blocks, mine):
            val = val + jnp.where((to == p)[None], v, 0.0)
        return val.reshape(32, 128).astype(BF16)

    for w, device in mates:
        ssend[w] = answer(w)
        pltpu.make_async_remote_copy(
            src_ref=ssend.at[w], dst_ref=srecv.at[m], send_sem=send.at[9], recv_sem=recv.at[9],
            device_id=device, device_id_type=MESH,
        ).start()
    srecv[m] = answer(m)
    own = jnp.zeros((32, 128), F32)
    for k in range(per):
        own = own + jnp.where(lax.rem(z, per) == k, blocks[k].reshape(32, 128), 0.0)
    xsend[...] = jnp.where(low[0:16], own[0:16], own[16:32])
    post(xmates, 10, lambda w: xsend, xrecv.at[x])
    xrecv[x] = xsend[...]

    land(grecv, pln, 8)
    packed = jnp.sum(grecv[...], axis=0)
    tall = jnp.concatenate([jnp.where(lane8 == q, packed, 0.0) for q in range(4)], axis=0)
    fold = jnp.where(
        jnp.bitwise_and(iota((128, 32), 0), 31) == iota((128, 32), 1), 1.0, 0.0
    )
    g0 = jnp.dot(tall, fold, precision=HI, preferred_element_type=F32)
    eye = jnp.where(iota((32, 32), 0) == iota((32, 32), 1), 1.0, 0.0)
    trace = jnp.sum(jnp.sum(g0 * eye, axis=1, keepdims=True), axis=0, keepdims=True)
    inv = 1.0 / jnp.sqrt(trace / rows_total + 1e-06)
    g = g0 * (inv * inv) / rows_total
    a0 = 1.5 * eye - 0.5 * g
    g2 = jnp.dot(g, g, precision=HI, preferred_element_type=F32)
    a0a0 = 2.25 * eye - 1.5 * g + 0.25 * g2
    a0g = 1.5 * g - 0.5 * g2
    move = inv * (1.5 * a0 - 0.5 * jnp.dot(a0a0, a0g, precision=HI, preferred_element_type=F32))
    mref[:, 0:32] = move

    land(srecv, pln, 9)
    land(xrecv, nx, 10)
    got = srecv[0].astype(F32)
    for w in range(1, pln):
        got = got + srecv[w].astype(F32)
    held = xrecv[lax.div(z, per)]
    held = jnp.concatenate([held, pltpu.roll(held, 64, 1)], axis=0)
    factor_ref[...] = jnp.dot(move, held[:, 0:64], precision=HI, preferred_element_type=F32)
    order = jnp.concatenate(
        [mref[pl.ds(0, 16, stride=2), :][:, 0:32], mref[pl.ds(1, 16, stride=2), :][:, 0:32]], axis=0
    )
    other = pltpu.roll(got, 64, 1)
    low16 = iota((16, 128), 1) < 64
    for t in range(2):
        both = jnp.where(low, got, other) if t == 0 else jnp.where(low, other, got)
        v = jnp.dot(order, both, precision=HI, preferred_element_type=F32)
        tf_ref[t] = jnp.where(low16, v[0:16], v[16:32]).astype(BF16)

    sent(tq, 2 * near + 1, 0)
    sent(tq, 2 * near, 13)
    sent(req, pln, 1)
    sent(gbuf, pln, 2)
    sent(wrecv, pln, 3)
    sent(lrecv, nz, 4)
    sent(precv, pln, 5)
    sent(zrecv, pln, 6)
    sent(yrecv, nz, 7)
    pltpu.make_async_copy(part, part, send.at[11]).wait()
    sent(grecv, pln, 8)
    sent(srecv, pln, 9)
    sent(xrecv, nx, 10)
    sent(goes, pln, 12)


def solution(mesh):
    nx = mesh.shape["rep"]
    nz = mesh.shape["tiles"] // YC
    pln = nx * YC
    qr = 32 // nx
    per = nz // nx

    def per_device(tiles, block_one, block_two, block_three, owner_map, u_one, u_two, u_three):
        rows_total = owner_map.shape[0] * tiles.shape[1]
        vm = pl.BlockSpec(memory_space=pltpu.VMEM)
        factor, tf = pl.pallas_call(
            functools.partial(kernel, nx, nz, rows_total),
            out_shape=(
                pltpu.VMEM((32, 64), F32),
                pltpu.VMEM((2, 16, 128), BF16),
            ),
            in_specs=[pl.BlockSpec(memory_space=pltpu.HBM)] * 8,
            out_specs=(vm, vm),
            scratch_shapes=[
                pltpu.SMEM((2,), jnp.int32),
                pltpu.SMEM((2,), jnp.int32),
                pltpu.SMEM((2,), jnp.int32),
                pltpu.SMEM((owner_map.shape[0],), jnp.int32),
                pltpu.VMEM(u_one.shape, F32),
                pltpu.VMEM(u_two.shape, BF16),
                pltpu.VMEM(u_three.shape, BF16),
                pltpu.VMEM((128, 4096), BF16),
                pltpu.VMEM((32, 256), F32),
                pltpu.VMEM((qr, 256), BF16),
                pltpu.VMEM((nz, qr, 256), BF16),
                pltpu.VMEM((pln, 16, 384), BF16),
                pltpu.VMEM((16, 384), BF16),
                pltpu.VMEM((pln, 16, 128), BF16),
                pltpu.VMEM((pln, 16, 128), BF16),
                pltpu.VMEM((32, 64, 128), F32),
                pltpu.VMEM((1024, 128), BF16),
                pltpu.VMEM((pln, 8, 128), F32),
                pltpu.VMEM((pln, 8, 128), BF16),
                pltpu.VMEM((pln, 8, 128), BF16),
                pltpu.VMEM((8, 128), BF16),
                pltpu.VMEM((nz, 8, 128), BF16),
                pltpu.VMEM((8, 128), BF16),
                pltpu.VMEM((pln, 8, 128), BF16),
                pltpu.VMEM((32, 128), BF16),
                pltpu.VMEM((pln, 32, 128), BF16),
                pltpu.VMEM((8, 128), F32),
                pltpu.VMEM((pln, 8, 128), F32),
                pltpu.VMEM((32, per // 2, 128), F32),
                pltpu.VMEM((nz, 32 // nz, per // 2, 128), F32),
                pltpu.VMEM((32, per // 2, 128), F32),
                pltpu.VMEM((8, 128), F32),
                pltpu.VMEM((pln, 8, 128), F32),
                pltpu.VMEM((pln, 32, 128), BF16),
                pltpu.VMEM((pln, 32, 128), BF16),
                pltpu.VMEM((16, 128), F32),
                pltpu.VMEM((nx, 16, 128), F32),
                pltpu.VMEM((32, 128), F32),
                pltpu.SemaphoreType.DMA((9,)),
                pltpu.SemaphoreType.DMA((14,)),
                pltpu.SemaphoreType.DMA((14,)),
            ],
            compiler_params=pltpu.CompilerParams(
                collective_id=0, has_side_effects=True, vmem_limit_bytes=60 << 20
            ),
            name="hooi_step",
        )(tiles, block_one, block_two, block_three, owner_map, u_one, u_two, u_three)
        return factor, tf.reshape(2, 2048)

    in_specs = (
        P(("tiles", "rep"), None, None),
        P(("tiles", "rep")),
        P(("tiles", "rep")),
        P(("tiles", "rep")),
        P(),
        P(None, "tiles"),
        P(None, "tiles"),
        P(),
    )
    out_specs = (P(None, "tiles"), P(("tiles", "rep"), None))
    return jax.shard_map(
        per_device, mesh=mesh, in_specs=in_specs, out_specs=out_specs, check_vma=False
    )
```

```python
import functools

import jax
import jax.numpy as jnp
from jax import lax
from jax.experimental import pallas as pl
from jax.experimental.pallas import tpu as pltpu
from jax.sharding import PartitionSpec as P

MESH = pl.DeviceIdType.MESH
YC = 8
F32 = jnp.float32
BF16 = jnp.bfloat16
HI = lax.Precision.HIGHEST


def iota(shape, dim):
    return lax.broadcasted_iota(jnp.int32, shape, dim)


def nt(a, b, precision=None):
    return lax.dot_general(
        a, b, (((1,), (1,)), ((), ())), precision=precision, preferred_element_type=F32
    )


def kernel(
    nx, nz, rows_total,
    tiles_ref, b1_hbm, b2_hbm, b3_hbm, owner_hbm, u1_hbm, u2_hbm, u3_hbm,
    factor_ref, tf_ref,
    b1_ref, b2_ref, b3_ref, owner_ref, u1_ref, u2_ref, u3_ref,
    tl, us, shq, tq, req, reqs, obuf, gbuf, ft, pt, wsend, whalf, wrecv, lsend, lrecv, psend, precv,
    zsend, zrecv, gosend, goes, ysend, yrecv, yall, gsend, grecv, ssend, srecv, xsend, xrecv, mref,
    tsem, send, recv,
):
    pln = nx * YC
    per = nz // nx
    qr = 32 // nx
    t_id = lax.axis_index("tiles")
    x = lax.axis_index("rep")
    z = lax.div(t_id, YC)
    yc = lax.rem(t_id, YC)
    m = x * YC + yc

    copies = [
        pltpu.make_async_copy(tiles_ref.at[t], tl.at[pl.ds(64 * t, 64)], tsem.at[t])
        for t in range(2)
    ]
    inputs = [
        pltpu.make_async_copy(src, dst, tsem.at[2 + n])
        for n, (src, dst) in enumerate(
            ((u2_hbm, u2_ref), (u1_hbm, u1_ref), (b1_hbm, b1_ref), (owner_hbm, owner_ref),
             (b2_hbm, b2_ref), (b3_hbm, b3_ref), (u3_hbm, u3_ref))
        )
    ]

    def far(d, n):
        return min(d, n - d)

    xs = [lax.rem(x + d, nx) for d in range(nx)]
    ys = [lax.rem(lax.div(yc, 2) + d, YC // 2) * 2 for d in range(YC // 2)]
    cs = [lax.rem(yc, 2), 1 - lax.rem(yc, 2)]
    steps = [
        (far(dx, nx) + far(dy, YC // 2), dx, dy, dc)
        for dx in range(nx) for dy in range(YC // 2) for dc in range(2)
    ]
    steps = sorted(steps, reverse=True)[:-1]
    mates = [
        (xs[dx] * YC + ys[dy] + cs[dc], {"tiles": z * YC + ys[dy] + cs[dc], "rep": xs[dx]})
        for _, dx, dy, dc in steps
    ]
    zs = [lax.rem(z + d, nz) for d in sorted(range(1, nz), key=lambda d: -far(d, nz))]
    peers = [(w, {"tiles": w * YC + yc, "rep": x}) for w in zs]
    xmates = [(w, {"tiles": t_id, "rep": w}) for w in xs[1:]]

    barrier = pltpu.get_barrier_semaphore()
    for c in inputs[:2]:
        c.start()
    for _, device in peers + mates:
        pl.semaphore_signal(barrier, inc=1, device_id=device, device_id_type=MESH)
    for c in inputs[2:] + copies:
        c.start()

    def post(who, phase, src, dst):
        for w, device in who:
            pltpu.make_async_remote_copy(
                src_ref=src(w), dst_ref=dst, send_sem=send.at[phase], recv_sem=recv.at[phase],
                device_id=device, device_id_type=MESH,
            ).start()

    def land(buf, n, phase):
        part = buf.at[pl.ds(0, n - 1)]
        pltpu.make_async_copy(part, part, recv.at[phase]).wait()

    def sent(buf, n, phase):
        part = buf.at[pl.ds(0, n - 1)]
        pltpu.make_async_copy(part, part, send.at[phase]).wait()

    for c in inputs[:2]:
        c.wait()
    us[:, pl.ds(0, 128)] = u2_ref[...].astype(F32)
    us[:, pl.ds(128, 64)] = jnp.zeros((32, 64), F32)
    us[:, pl.ds(192, 64)] = u1_ref[...]
    shq[...] = us[pl.ds(pl.multiple_of(x * qr, qr), qr), :].astype(BF16)
    pl.semaphore_wait(barrier, pln + nz - 2)
    post(peers, 0, lambda w: shq, tq.at[z])

    for c in inputs[2:]:
        c.wait()
    b2 = [b2_ref[t] for t in range(2)]
    b3 = [b3_ref[t] for t in range(2)]
    pos = [owner_ref[b1_ref[t]] for t in range(2)]

    r16 = iota((16, 128), 0)
    l16 = iota((16, 128), 1)

    def ask(q0, q1):
        want = jnp.where(r16 < qr, q0 * qr, q1 * qr - qr) + r16
        return jnp.where(l16 == want, 1.0, 0.0)

    ask_two = ask(lax.shift_right_logical(b2[0], 4), lax.shift_right_logical(b2[1], 4))
    odd = jnp.where(r16 < qr, lax.rem(b2[0], 2), lax.rem(b2[1], 2)) == 1
    reqs[:, 0:128] = jnp.where(odd, 0.0, ask_two).astype(BF16)
    reqs[:, 128:256] = jnp.where(odd, ask_two, 0.0).astype(BF16)
    reqs[:, 256:384] = ask(
        lax.shift_right_logical(pos[0], 3), lax.shift_right_logical(pos[1], 3)
    ).astype(BF16)
    post(mates, 1, lambda w: reqs, req.at[m])
    tq[z] = shq[...]
    req[m] = reqs[...]
    gosend[...] = jnp.where(iota((8, 128), 1) < 64, pos[0], pos[1]).astype(F32)
    goes[m] = gosend[...]

    lane128 = iota((32, 128), 1)
    spread = jnp.where(iota((256, 32), 0) // 8 == iota((256, 32), 1), 1.0, 0.0).astype(BF16)
    diag = []
    for t in range(2):
        chunk = jnp.zeros((32, 128), F32)
        for q in range(8):
            part = u3_ref[:, q * 128 : (q + 1) * 128].astype(F32)
            chunk = chunk + jnp.where(lax.shift_right_logical(b3[t], 1) == q, part, 0.0)
        swapped = pltpu.roll(chunk, 64, 1)
        odd = lax.rem(b3[t], 2) == 1
        twice = jnp.where((lane128 < 64) != odd, chunk, swapped)
        wide = jnp.dot(spread, twice.astype(BF16), preferred_element_type=F32)
        row = lax.rem(iota((256, 128), 0), 8)
        half = jnp.where(iota((256, 128), 1) < 64, 0, 1)
        diag.append(
            jnp.concatenate(
                [jnp.where(row == half + 2 * q, wide, 0.0).astype(BF16) for q in range(4)], axis=1
            )
        )
    for c in copies:
        c.wait()
    low256 = iota((256, 128), 1) < 64
    for jc in range(8):
        block = tl[:, jc * 512 : (jc + 1) * 512]
        out = jnp.where(low256, nt(diag[0], block), nt(diag[1], block))
        ft[:, jc * 8 : (jc + 1) * 8, :] = out.reshape(32, 8, 128)

    land(tq, nz, 0)
    land(req, pln, 1)
    table = tq[...].astype(F32).reshape(nz * qr, 256)
    halves = jnp.concatenate([table[:, 0:128], pltpu.roll(table[:, 0:128], 64, 1)], axis=0)
    two_part = jnp.dot(
        req[:, :, 0:256].reshape(pln * 16, 256), halves.astype(BF16), preferred_element_type=F32
    )
    one_part = jnp.dot(
        req[:, :, 256:384].reshape(pln * 16, 128), table[:, 128:256].astype(BF16),
        preferred_element_type=F32,
    )
    both = jnp.where(iota((pln * 16, 128), 1) < 64, two_part, one_part)
    obuf[...] = both.reshape(pln, 16, 128).astype(BF16)
    post(mates, 2, lambda w: obuf.at[w], gbuf.at[m])
    gbuf[m] = obuf[m]
    land(gbuf, pln, 2)

    held_two = [lax.rem(lax.shift_right_logical(b, 1), YC) for b in b2]
    held_one = [lax.rem(p, YC) for p in pos]
    holder = jnp.where(
        l16 < 64,
        jnp.where(r16 < 8, held_two[0], held_two[1]),
        jnp.where(r16 < 8, held_one[0], held_one[1]),
    )
    parts = []
    for xx in range(nx):
        acc = jnp.zeros((16, 128), F32)
        for cc in range(YC):
            acc = acc + jnp.where(holder == cc, gbuf[xx * YC + cc].astype(F32), 0.0)
        parts.append(acc)
    low = lane128 < 64
    picked = [jnp.concatenate([p[t * 8 : t * 8 + 8] for p in parts], axis=0) for t in range(2)]
    u2 = jnp.concatenate(picked, axis=0)[:, 0:64].astype(BF16)
    readers = jnp.where(low, pltpu.roll(picked[0], 64, 1), picked[1]).astype(BF16)

    for s in range(32):
        d = jnp.dot(u2, ft[s].astype(BF16), preferred_element_type=F32)
        pt[s * 32 : (s + 1) * 32, :] = jnp.where(low, d[0:32], d[32:64]).astype(BF16)

    w_part = nt(readers, pt[...])
    for q in range(8):
        wsend[:, q, :] = w_part[:, q * 128 : (q + 1) * 128]
    whalf[...] = wsend[...].astype(BF16)
    post(mates, 3, lambda w: whalf.at[w], wrecv.at[m])
    wrecv[m] = whalf[m]
    land(wrecv, pln, 3)
    lsend[...] = jnp.sum(wrecv[...].astype(F32), axis=0).astype(BF16)
    post(peers, 4, lambda w: lsend, lrecv.at[z])
    lrecv[z] = lsend[...]
    post(mates, 12, lambda w: gosend, goes.at[m])
    land(lrecv, nz, 4)
    psend[...] = jnp.sum(lrecv[...].astype(F32), axis=0).astype(BF16)
    post(mates, 5, lambda w: psend, precv.at[m])
    precv[m] = psend[...]
    land(precv, pln, 5)
    wsend[...] = precv[...].astype(F32)
    project = jnp.concatenate([wsend[:, q, :].astype(BF16) for q in range(8)], axis=1)

    zsend[...] = jnp.dot(project, pt[...], preferred_element_type=F32).astype(BF16)
    post(mates, 6, lambda w: zsend, zrecv.at[m])
    zrecv[m] = zsend[...]
    land(zrecv, pln, 6)
    mine = [((x * per + k) * YC + yc).astype(F32) for k in range(per)]
    land(goes, pln, 12)
    sums = [jnp.zeros((4, 8, 128), F32) for _ in range(per)]
    for w in range(pln):
        to = goes[w]
        val = zrecv[w].astype(F32).reshape(4, 8, 128)
        sums = [v + jnp.where((to == p)[None], val, 0.0) for v, p in zip(sums, mine)]
    sums = [v.reshape(32, 128) for v in sums]
    sums = [v + pltpu.roll(v, 64, 1) for v in sums]
    half = per // 2
    for h in range(half):
        ysend[:, h, :] = jnp.where(low, sums[2 * h], sums[2 * h + 1])
    rz = 32 // nz

    def slab(ref, w):
        return ref.at[pl.ds(w * rz, rz)]

    post(peers, 7, lambda w: slab(ysend, w), yrecv.at[z])
    yrecv[z] = ysend[pl.ds(z * rz, rz)]
    land(yrecv, nz, 7)
    yall[pl.ds(z * rz, rz)] = jnp.sum(yrecv[...], axis=0)
    post(peers, 11, lambda w: slab(yall, z), slab(yall, z))
    part = yall.at[pl.ds(0, rz * (nz - 1))]
    pltpu.make_async_copy(part, part, recv.at[11]).wait()
    total = jnp.concatenate([yall[:, h, :] for h in range(half)], axis=1)

    rounded = total.astype(BF16)
    gw = nt(rounded, jnp.concatenate([rounded] * 4, axis=0))
    lane8 = lax.shift_right_logical(iota((8, 128), 1), 5)
    packed = jnp.zeros((8, 128), F32)
    for q in range(4):
        packed = packed + jnp.where(lane8 == q, gw[q * 8 : q * 8 + 8], 0.0)
    gsend[...] = packed
    post(mates, 8, lambda w: gsend, grecv.at[m])
    grecv[m] = packed
    blocks = []
    for k in range(per):
        pair = total[:, (k // 2) * 128 : (k // 2) * 128 + 128]
        other = pltpu.roll(pair, 64, 1)
        blocks.append(jnp.where(low, pair, other) if k % 2 == 0 else jnp.where(low, other, pair))
    blocks = [v.reshape(4, 8, 128) for v in blocks]

    def answer(w):
        to = goes[w]
        val = jnp.zeros((4, 8, 128), F32)
        for v, p in zip(blocks, mine):
            val = val + jnp.where((to == p)[None], v, 0.0)
        return val.reshape(32, 128).astype(BF16)

    for w, device in mates:
        ssend[w] = answer(w)
        pltpu.make_async_remote_copy(
            src_ref=ssend.at[w], dst_ref=srecv.at[m], send_sem=send.at[9], recv_sem=recv.at[9],
            device_id=device, device_id_type=MESH,
        ).start()
    srecv[m] = answer(m)
    own = jnp.zeros((32, 128), F32)
    for k in range(per):
        own = own + jnp.where(lax.rem(z, per) == k, blocks[k].reshape(32, 128), 0.0)
    xsend[...] = jnp.where(low[0:16], own[0:16], own[16:32])
    post(xmates, 10, lambda w: xsend, xrecv.at[x])
    xrecv[x] = xsend[...]

    land(grecv, pln, 8)
    packed = jnp.sum(grecv[...], axis=0)
    tall = jnp.concatenate([jnp.where(lane8 == q, packed, 0.0) for q in range(4)], axis=0)
    fold = jnp.where(
        jnp.bitwise_and(iota((128, 32), 0), 31) == iota((128, 32), 1), 1.0, 0.0
    )
    g0 = jnp.dot(tall, fold, precision=HI, preferred_element_type=F32)
    eye = jnp.where(iota((32, 32), 0) == iota((32, 32), 1), 1.0, 0.0)
    trace = jnp.sum(jnp.sum(g0 * eye, axis=1, keepdims=True), axis=0, keepdims=True)
    inv = 1.0 / jnp.sqrt(trace / rows_total + 1e-06)
    g = g0 * (inv * inv) / rows_total
    a0 = 1.5 * eye - 0.5 * g
    g2 = jnp.dot(g, g, precision=HI, preferred_element_type=F32)
    a0a0 = 2.25 * eye - 1.5 * g + 0.25 * g2
    a0g = 1.5 * g - 0.5 * g2
    move = inv * (1.5 * a0 - 0.5 * jnp.dot(a0a0, a0g, precision=HI, preferred_element_type=F32))
    mref[:, 0:32] = move

    land(srecv, pln, 9)
    land(xrecv, nx, 10)
    got = srecv[0].astype(F32)
    for w in range(1, pln):
        got = got + srecv[w].astype(F32)
    held = xrecv[lax.div(z, per)]
    held = jnp.concatenate([held, pltpu.roll(held, 64, 1)], axis=0)
    factor_ref[...] = jnp.dot(move, held[:, 0:64], precision=HI, preferred_element_type=F32)
    order = jnp.concatenate(
        [mref[pl.ds(0, 16, stride=2), :][:, 0:32], mref[pl.ds(1, 16, stride=2), :][:, 0:32]], axis=0
    )
    other = pltpu.roll(got, 64, 1)
    low16 = iota((16, 128), 1) < 64
    for t in range(2):
        both = jnp.where(low, got, other) if t == 0 else jnp.where(low, other, got)
        v = jnp.dot(order, both, precision=HI, preferred_element_type=F32)
        tf_ref[t] = jnp.where(low16, v[0:16], v[16:32]).astype(BF16)

    sent(tq, nz, 0)
    sent(req, pln, 1)
    sent(gbuf, pln, 2)
    sent(wrecv, pln, 3)
    sent(lrecv, nz, 4)
    sent(precv, pln, 5)
    sent(zrecv, pln, 6)
    sent(yrecv, nz, 7)
    pltpu.make_async_copy(part, part, send.at[11]).wait()
    sent(grecv, pln, 8)
    sent(srecv, pln, 9)
    sent(xrecv, nx, 10)
    sent(goes, pln, 12)


def solution(mesh):
    nx = mesh.shape["rep"]
    nz = mesh.shape["tiles"] // YC
    pln = nx * YC
    qr = 32 // nx
    per = nz // nx

    def per_device(tiles, block_one, block_two, block_three, owner_map, u_one, u_two, u_three):
        rows_total = owner_map.shape[0] * tiles.shape[1]
        vm = pl.BlockSpec(memory_space=pltpu.VMEM)
        factor, tf = pl.pallas_call(
            functools.partial(kernel, nx, nz, rows_total),
            out_shape=(
                pltpu.VMEM((32, 64), F32),
                pltpu.VMEM((2, 16, 128), BF16),
            ),
            in_specs=[pl.BlockSpec(memory_space=pltpu.HBM)] * 8,
            out_specs=(vm, vm),
            scratch_shapes=[
                pltpu.SMEM((2,), jnp.int32),
                pltpu.SMEM((2,), jnp.int32),
                pltpu.SMEM((2,), jnp.int32),
                pltpu.SMEM((owner_map.shape[0],), jnp.int32),
                pltpu.VMEM(u_one.shape, F32),
                pltpu.VMEM(u_two.shape, BF16),
                pltpu.VMEM(u_three.shape, BF16),
                pltpu.VMEM((128, 4096), BF16),
                pltpu.VMEM((32, 256), F32),
                pltpu.VMEM((qr, 256), BF16),
                pltpu.VMEM((nz, qr, 256), BF16),
                pltpu.VMEM((pln, 16, 384), BF16),
                pltpu.VMEM((16, 384), BF16),
                pltpu.VMEM((pln, 16, 128), BF16),
                pltpu.VMEM((pln, 16, 128), BF16),
                pltpu.VMEM((32, 64, 128), F32),
                pltpu.VMEM((1024, 128), BF16),
                pltpu.VMEM((pln, 8, 128), F32),
                pltpu.VMEM((pln, 8, 128), BF16),
                pltpu.VMEM((pln, 8, 128), BF16),
                pltpu.VMEM((8, 128), BF16),
                pltpu.VMEM((nz, 8, 128), BF16),
                pltpu.VMEM((8, 128), BF16),
                pltpu.VMEM((pln, 8, 128), BF16),
                pltpu.VMEM((32, 128), BF16),
                pltpu.VMEM((pln, 32, 128), BF16),
                pltpu.VMEM((8, 128), F32),
                pltpu.VMEM((pln, 8, 128), F32),
                pltpu.VMEM((32, per // 2, 128), F32),
                pltpu.VMEM((nz, 32 // nz, per // 2, 128), F32),
                pltpu.VMEM((32, per // 2, 128), F32),
                pltpu.VMEM((8, 128), F32),
                pltpu.VMEM((pln, 8, 128), F32),
                pltpu.VMEM((pln, 32, 128), BF16),
                pltpu.VMEM((pln, 32, 128), BF16),
                pltpu.VMEM((16, 128), F32),
                pltpu.VMEM((nx, 16, 128), F32),
                pltpu.VMEM((32, 128), F32),
                pltpu.SemaphoreType.DMA((9,)),
                pltpu.SemaphoreType.DMA((13,)),
                pltpu.SemaphoreType.DMA((13,)),
            ],
            compiler_params=pltpu.CompilerParams(
                collective_id=0, has_side_effects=True, vmem_limit_bytes=60 << 20
            ),
            name="hooi_step",
        )(tiles, block_one, block_two, block_three, owner_map, u_one, u_two, u_three)
        return factor, tf.reshape(2, 2048)

    in_specs = (
        P(("tiles", "rep"), None, None),
        P(("tiles", "rep")),
        P(("tiles", "rep")),
        P(("tiles", "rep")),
        P(),
        P(None, "tiles"),
        P(None, "tiles"),
        P(),
    )
    out_specs = (P(None, "tiles"), P(("tiles", "rep"), None))
    return jax.shard_map(
        per_device, mesh=mesh, in_specs=in_specs, out_specs=out_specs, check_vma=False
    )
```
